256 devices in a mesh: gx: 32 (over y, z_lo, core), gy: 8 (over z_hi, x).
Axes of the slice: x: 4, y: 4, z: 8 (z_hi: 2, z_lo: 4; z = z_hi * 4 + z_lo), core: 2. Of those that a mesh axis runs over, the one named last changes fastest.
Arguments:
- features: bfloat16 [32, 8, 3, 512, 192], P('gx', 'gy'), may hold values from -6 to 6
- weight: bfloat16 [5184, 192], replicated, may hold values from -0.078125 to 0.078125
- cotangent: bfloat16 [32, 8, 3, 64, 192], P('gx', 'gy'), may hold values from -6 to 6
- valid: int32 [32, 8, 3], P('gx', 'gy'), may hold values from 0 to 1, as said below
- local_rules: int32 [32, 8, 2, 12], P('gx', 'gy'), may hold values from 0 to 3, as said below
- local_codes: int32 [32, 8, 12], P('gx', 'gy'), may hold values from 0 to 7
- remote_rules: int32 [32, 8, 2, 3, 3], P('gx', 'gy'), may hold values from 0 to 3, as said below
- remote_codes: int32 [32, 8, 3, 3], P('gx', 'gy'), may hold values from 1 to 7, as said below
Outputs:
- output: bfloat16 [32, 8, 3, 64, 192], P('gx', 'gy')
- features_grad: bfloat16 [32, 8, 3, 512, 192], P('gx', 'gy')
- weight_grad: float32 [5184, 192], P('gx')
The draws below stay inside these ranges and needn't reach their ends.
Inputs may be any that keep to these rules, and one draw needn't show every extreme that they name: `valid`: 1 marks a live brick slot; on each device the live slots come first and at least one slot is live. `local_rules`: entry [., ., 0, e] is a source slot and [., ., 1, e] a target slot of the same device; a target 3 marks an empty entry; non-empty entries name live slots. `remote_rules`: class m (third dimension) entry: a source slot on this device and a target slot on the device one step higher along gx (m = 0), along gy (m = 1) or along both (m = 2); a target 3 marks an empty entry; non-empty entries name live slots; devices at the upper end of an axis have no non-empty entries in the classes that cross it. `remote_codes`: the offset k mod 2 is 1 in classes 0 and 2, and the offset (k // 2) mod 2 is 1 in classes 1 and 2.
All inputs are finite; a program needn't handle non-finite values.
Results may differ from the reference program's by a relative error of at most 0.0045.
Values may be sent and summed in bfloat16 or wider, within the bound.
No kernel may reach another device: no remote copies, remote signals or barrier semaphores. Data moves between devices by JAX's collectives and lax.ppermute only.
A program may use at most 128 MiB of HBM per device.

```python
import jax
import jax.numpy as jnp
import numpy as np
from jax import lax

C = 192
NB = 3
RL = 12
RR = 3
GRID_X = 32
GRID_Y = 8


def live_counts(key):
    return jax.random.randint(jax.random.fold_in(key, 11), (GRID_X, GRID_Y), 1, NB + 1)


def draw_valid(key, part):
    live_count = live_counts(key)
    slot_ids = jnp.arange(NB, dtype=jnp.int32)[None, None, :]
    return (slot_ids < live_count[..., None]).astype(jnp.int32)


def local_plan(key):
    live_count = live_counts(key)
    slot_ids = jnp.broadcast_to(jnp.arange(RL, dtype=jnp.int32)[None, None, :], (GRID_X, GRID_Y, RL))
    own_slot = slot_ids < NB
    extra_count = jax.random.randint(jax.random.fold_in(key, 21), (GRID_X, GRID_Y), NB, 3 * NB)
    extra_live = (slot_ids >= NB) & (slot_ids < NB + extra_count[..., None])
    random_source = jax.random.randint(jax.random.fold_in(key, 22), (GRID_X, GRID_Y, RL), 0, live_count[..., None])
    random_target = jax.random.randint(jax.random.fold_in(key, 23), (GRID_X, GRID_Y, RL), 0, live_count[..., None])
    own_live = own_slot & (slot_ids < live_count[..., None])
    source = jnp.where(own_slot, slot_ids, jnp.where(extra_live, random_source, 0))
    target = jnp.where(own_live, slot_ids, jnp.where(extra_live, random_target, NB))
    code_list = jnp.where(own_slot, 0, jax.random.randint(jax.random.fold_in(key, 24), (GRID_X, GRID_Y, RL), 1, 8))
    return (jnp.stack([source, target], axis=2).astype(jnp.int32), code_list.astype(jnp.int32))


def draw_local_rules(key, part):
    return local_plan(key)[0]


def draw_local_codes(key, part):
    return local_plan(key)[1]


def remote_plan(key):
    live_count = live_counts(key)
    above_x = jnp.roll(live_count, -1, axis=0)
    above_y = jnp.roll(live_count, -1, axis=1)
    above_both = jnp.roll(above_x, -1, axis=1)
    dest_live = jnp.stack([above_x, above_y, above_both], axis=2)
    lower_x = jnp.broadcast_to(jnp.arange(GRID_X)[:, None] < GRID_X - 1, (GRID_X, GRID_Y))
    lower_y = jnp.broadcast_to(jnp.arange(GRID_Y)[None, :] < GRID_Y - 1, (GRID_X, GRID_Y))
    reach = jnp.stack([lower_x, lower_y, lower_x & lower_y], axis=2).astype(jnp.int32)
    rule_count = jax.random.randint(jax.random.fold_in(key, 31), (GRID_X, GRID_Y, 3), 1, RR + 1) * reach
    slot_ids = jnp.arange(RR, dtype=jnp.int32)[None, None, None, :]
    live_rule = slot_ids < rule_count[..., None]
    shape_all = (GRID_X, GRID_Y, 3, RR)
    random_source = jax.random.randint(jax.random.fold_in(key, 32), shape_all, 0, live_count[..., None, None])
    random_target = jax.random.randint(jax.random.fold_in(key, 33), shape_all, 0, dest_live[..., None])
    source = jnp.where(live_rule, random_source, 0)
    target = jnp.where(live_rule, random_target, NB)
    free_x = jax.random.randint(jax.random.fold_in(key, 34), shape_all, 0, 2)
    free_y = jax.random.randint(jax.random.fold_in(key, 35), shape_all, 0, 2)
    free_z = jax.random.randint(jax.random.fold_in(key, 36), shape_all, 0, 2)
    class_ids = jnp.arange(3, dtype=jnp.int32)[None, None, :, None]
    offset_x = jnp.where(class_ids == 1, free_x, 1)
    offset_y = jnp.where(class_ids == 0, free_y, 1)
    code_list = offset_x + 2 * offset_y + 4 * free_z
    return (jnp.stack([source, target], axis=2).astype(jnp.int32), code_list.astype(jnp.int32))


def draw_remote_rules(key, part):
    return remote_plan(key)[0]


def draw_remote_codes(key, part):
    return remote_plan(key)[1]


def levels(own_key, shape, cuts, smallest, largest):
    gain = 1.0
    for dim, parts in cuts:
        heights = jax.random.uniform(jax.random.fold_in(jax.random.fold_in(own_key, 6), dim), (parts,), jnp.float32, smallest / len(cuts), largest / len(cuts))
        gain = gain * jnp.repeat(jnp.exp(heights), shape[dim] // parts).reshape((-1,) + (1,) * (len(shape) - 1 - dim))
    return gain


def noise(own_key, dims, deviation, limit, shards=(), held_as=jnp.bfloat16):
    factor_of = levels(own_key, dims, shards, -0.22, 0.18) if shards else 1.0
    array = jax.random.normal(own_key, dims, jnp.float32) * deviation * factor_of
    return jnp.minimum(jnp.maximum(array, -limit), limit).astype(held_as)


def setup_inputs(seed: int = 0) -> dict:
    streams_of = jax.random.split(jax.random.key(seed), 9)
    features = noise(streams_of[0], (GRID_X, GRID_Y, NB, 512, C), 1.0, 6.0, ((0, 32), (1, 8)))
    weight = noise(streams_of[1], (27 * C, C), (27 * C) ** -0.5, 0.078125)
    cotangent = noise(streams_of[2], (GRID_X, GRID_Y, NB, 64, C), 1.0, 6.0, ((0, 32), (1, 8)))
    valid = draw_valid(jax.random.fold_in(streams_of[8], 71), 0)
    local_rules = draw_local_rules(jax.random.fold_in(streams_of[8], 71), 0)
    local_codes = draw_local_codes(jax.random.fold_in(streams_of[8], 71), 0)
    remote_rules = draw_remote_rules(jax.random.fold_in(streams_of[8], 71), 0)
    remote_codes = draw_remote_codes(jax.random.fold_in(streams_of[8], 71), 0)
    return {"features": features, "weight": weight, "cotangent": cotangent, "valid": valid, "local_rules": local_rules, "local_codes": local_codes, "remote_rules": remote_rules, "remote_codes": remote_codes}


def offset_table(row_x, row_y, row_z):
    code_list = np.arange(8)[:, None]
    step_x = code_list % 2
    step_y = (code_list // 2) % 2
    step_z = code_list // 4
    inside = ((step_x == 0) | (row_x[None, :] == 0)) & ((step_y == 0) | (row_y[None, :] == 0)) & ((step_z == 0) | (row_z[None, :] == 0))
    source_row = (row_x[None, :] + 4 * step_x) * 25 + (row_y[None, :] + 4 * step_y) * 5 + row_z[None, :] + 4 * step_z
    return np.where(inside, source_row, 125).astype(np.int32)


def full_table():
    voxel_ids = np.arange(64)
    return offset_table(voxel_ids // 16, (voxel_ids // 4) % 4, voxel_ids % 4)


def brick_patches(one_brick):
    channels = one_brick.shape[-1]
    cube = one_brick.reshape(8, 8, 8, channels)
    padded = jnp.pad(cube, ((1, 2), (1, 2), (1, 2), (0, 0)))
    tap_list = []
    for along_x in range(3):
        for along_y in range(3):
            for along_z in range(3):
                tap_list.append(padded[along_x:along_x + 9:2, along_y:along_y + 9:2, along_z:along_z + 9:2, :])
    return jnp.stack(tap_list, axis=3).reshape(125, 27 * channels)


def brick_fold(patch_grads, channels):
    tap_grads = patch_grads.reshape(5, 5, 5, 27, channels)
    padded = jnp.zeros((11, 11, 11, channels), jnp.float32)
    tap_index = 0
    for along_x in range(3):
        for along_y in range(3):
            for along_z in range(3):
                padded = padded.at[along_x:along_x + 9:2, along_y:along_y + 9:2, along_z:along_z + 9:2, :].add(tap_grads[:, :, :, tap_index, :])
                tap_index = tap_index + 1
    return padded[1:9, 1:9, 1:9, :].reshape(512, channels)


def reference(features, weight, cotangent, valid, local_rules, local_codes, remote_rules, remote_codes):
    channels = features.shape[-1]
    live_mask = valid.astype(jnp.bfloat16)[..., None, None]
    live_float = valid.astype(jnp.float32)[..., None, None]
    masked = features * live_mask
    tile_bricks = masked.reshape(GRID_X * GRID_Y, NB, 512, channels)

    def forward_tile(tile):
        patches = jax.vmap(brick_patches)(tile).reshape(NB * 125, 27 * channels)
        return jnp.dot(patches, weight, preferred_element_type=jnp.float32).reshape(NB, 125, channels)

    partials = lax.map(forward_tile, tile_bricks).reshape(GRID_X * GRID_Y * NB, 125, channels)
    zero_rows = jnp.zeros((partials.shape[0], 1, channels), jnp.float32)
    padded = jnp.concatenate([partials, zero_rows], axis=1).reshape(GRID_X, GRID_Y, NB, 126, channels)
    full_map = jnp.asarray(full_table())
    column_x = jnp.arange(GRID_X, dtype=jnp.int32)[:, None, None]
    column_y = jnp.arange(GRID_Y, dtype=jnp.int32)[None, :, None]
    rule_sets = [(local_rules[:, :, 0], local_rules[:, :, 1], local_codes, 0, 0)]
    for rule_class, steps_xy in enumerate(((1, 0), (0, 1), (1, 1))):
        rule_sets.append((remote_rules[:, :, 0, rule_class], remote_rules[:, :, 1, rule_class], remote_codes[:, :, rule_class], steps_xy[0], steps_xy[1]))
    totals = jnp.zeros((GRID_X, GRID_Y, NB + 1, 64, channels), jnp.float32)
    placed = []
    for sources, targets, code_list, step_x, step_y in rule_sets:
        dest_x = jnp.broadcast_to(column_x + step_x, sources.shape)
        dest_y = jnp.broadcast_to(column_y + step_y, sources.shape)
        inside = (dest_x < GRID_X) & (dest_y < GRID_Y)
        kept_target = jnp.where(inside, targets, NB).astype(jnp.int32)
        dest_x = jnp.minimum(dest_x, GRID_X - 1).astype(jnp.int32)
        dest_y = jnp.minimum(dest_y, GRID_Y - 1).astype(jnp.int32)
        row_index = full_map[code_list]
        anchor_x = jnp.broadcast_to(column_x, sources.shape)[..., None]
        anchor_y = jnp.broadcast_to(column_y, sources.shape)[..., None]
        pieces = padded[anchor_x, anchor_y, sources[..., None], row_index]
        totals = totals.at[dest_x, dest_y, kept_target].add(pieces)
        placed.append((anchor_x, anchor_y, sources, row_index, dest_x, dest_y, kept_target))
    output = (totals[:, :, :NB] * live_float).astype(jnp.bfloat16)

    grad_out = (cotangent * live_mask).astype(jnp.float32)
    grad_pad = jnp.concatenate([grad_out, jnp.zeros((GRID_X, GRID_Y, 1, 64, channels), jnp.float32)], axis=2)
    grad_rows = jnp.zeros((GRID_X, GRID_Y, NB, 126, channels), jnp.float32)
    for anchor_x, anchor_y, sources, row_index, dest_x, dest_y, kept_target in placed:
        grad_rows = grad_rows.at[anchor_x, anchor_y, sources[..., None], row_index].add(grad_pad[dest_x, dest_y, kept_target])
    grad_rounded = grad_rows[:, :, :, :125].astype(jnp.bfloat16).reshape(GRID_X * GRID_Y, NB * 125, channels)

    def fold_one(patch_grads):
        return brick_fold(patch_grads, channels)

    def backward_tile(running, inputs):
        tile, tile_grads = inputs
        patches = jax.vmap(brick_patches)(tile).reshape(NB * 125, 27 * channels)
        patch_grads = jnp.dot(tile_grads, weight.T, preferred_element_type=jnp.float32).reshape(NB, 125, 27 * channels)
        running = running + jnp.dot(patches.T, tile_grads, preferred_element_type=jnp.float32)
        return running, jax.vmap(fold_one)(patch_grads)

    weight_grad, folded = lax.scan(backward_tile, jnp.zeros((27 * channels, channels), jnp.float32), (tile_bricks, grad_rounded))
    features_grad = (folded.reshape(GRID_X, GRID_Y, NB, 512, channels) * live_float).astype(jnp.bfloat16)
    return output, features_grad, weight_grad
```

```python
import functools

import jax
import jax.numpy as jnp
from jax import lax
from jax.experimental import pallas as pl
from jax.experimental.pallas import tpu as pltpu
from jax.sharding import PartitionSpec as P

INTERPRET = False
BF = jnp.bfloat16
F32 = jnp.float32
VM = pltpu.MemorySpace.VMEM
SM = pltpu.MemorySpace.SMEM

PARITY = (1, 0, 1)
SHIFT = (1, 0, 0)
TAPS = [(e, f, g) for e in range(3) for f in range(3) for g in range(3)]


def tap_parity(tap):
    return PARITY[tap[0]] * 4 + PARITY[tap[1]] * 2 + PARITY[tap[2]]


def tap_shift(tap):
    return SHIFT[tap[0]] + 2 * SHIFT[tap[1]] + 4 * SHIFT[tap[2]]


def call(kernel, outs, args, spaces, scratch, flops, name, limit=4):
    nbytes = sum(a.size * a.dtype.itemsize for a in args)
    return pl.pallas_call(
        kernel,
        out_shape=outs,
        in_specs=[pl.BlockSpec(memory_space=s) for s in spaces],
        out_specs=jax.tree.map(lambda _: pl.BlockSpec(memory_space=VM), outs),
        scratch_shapes=scratch,
        compiler_params=pltpu.CompilerParams(vmem_limit_bytes=limit << 20),
        cost_estimate=pl.CostEstimate(flops=flops, bytes_accessed=nbytes, transcendentals=0),
        interpret=INTERPRET,
        name=name,
    )(*args)


def split_kernel(valid, feat, out, low, high):
    for slot in range(3):
        live = valid[0, 0, slot].astype(F32)
        for x in range(8):
            rows = feat[0, 0, slot, x * 64 : (x + 1) * 64, :].astype(F32) * live
            start = slot * 512 + ((x % 2) * 4 + x // 2) * 64
            low[start : start + 64, :] = rows[:, :128]
            high[start : start + 64, 0:64] = rows[:, 128:]
    for slot in range(3):
        for a in range(2):
            for b in range(2):
                for z in range(8):
                    take = pl.ds(slot * 512 + a * 256 + b * 8 + z, 16, stride=16)
                    row = slot * 64 + (z // 2) * 16
                    par = a * 4 + b * 2 + z % 2
                    out[par, row : row + 16, 0:128] = low[take, :].astype(BF)
                    out[par, row : row + 16, 128:192] = high[take, :][:, 0:64].astype(BF)


def row_ids():
    return lax.broadcasted_iota(jnp.int32, (64, 192), 0)


def gather_shift(first, second, axis):
    if axis == 2:
        return jnp.concatenate([first[16:], second[:16]], axis=0)
    step = 4 if axis == 0 else 1
    at = row_ids() // step % 4
    up = pltpu.roll(first, 64 - step, 0)
    wrap = pltpu.roll(second, 3 * step, 0)
    return jnp.where(at == 3, wrap, up)


def to_cube_order(cube, low, high):
    low[...] = cube[:, :128]
    high[:, 0:64] = cube[:, 128:]
    parts = []
    for r in range(4):
        take = pl.ds(r, 16, stride=4)
        parts.append(jnp.concatenate([low[take, :], high[take, :][:, 0:64]], axis=1))
    return jnp.concatenate(parts, axis=0)


def weight_kernel(
    lrules, lcodes, rrules, rcodes, split, cot, cot_x, cot_y, cot_xy,
    keep, send, shifts, cubes, grads, low, high, total,
):
    zero = jnp.zeros((64, 192), F32)
    for group, ref in enumerate((cot, cot_x, cot_y, cot_xy)):
        for slot in range(3):
            rows = ref[0, 0, slot].astype(F32)
            cubes[group * 4 + slot] = to_cube_order(rows, low, high)
        cubes[group * 4 + 3] = zero
    for entry in range(32):
        grads[entry] = zero
    for e in range(12):
        at = lrules[0, 0, 0, e] * 8 + lcodes[0, 0, e]
        grads[at] += cubes[lrules[0, 0, 1, e]]
    for m in range(3):
        for e in range(3):
            at = rrules[0, 0, 0, m, e] * 8 + rcodes[0, 0, m, e]
            grads[at] += cubes[(m + 1) * 4 + rrules[0, 0, 1, m, e]]
    for slot in range(3):
        level = {}
        for u in range(2):
            for v in range(2):
                first = grads[slot * 8 + u + 2 * v]
                second = grads[slot * 8 + u + 2 * v + 4]
                level[u, v, 0] = first
                level[u, v, 1] = gather_shift(first, second, 2)
        after = {}
        for v in range(2):
            for w in range(2):
                after[0, v, w] = level[0, v, w]
                after[1, v, w] = gather_shift(level[0, v, w], level[1, v, w], 0)
        for u in range(2):
            for w in range(2):
                rows = slice(slot * 64, slot * 64 + 64)
                shifts[u + 4 * w, rows, :] = after[u, 0, w].astype(BF)
                shifts[u + 2 + 4 * w, rows, :] = gather_shift(
                    after[u, 0, w], after[u, 1, w], 1
                ).astype(BF)
    for index, tap in enumerate(TAPS):
        total[index * 192 : (index + 1) * 192, :] = lax.dot_general(
            split[tap_parity(tap)],
            shifts[tap_shift(tap)],
            (((0,), (0,)), ((), ())),
            preferred_element_type=F32,
        )
    here = lax.axis_index("gx")
    core = here % 2
    for m in range(16):
        pair = (here // 2) ^ m
        for own in range(2):
            block = pair * 2 + (core if own else 1 - core)
            start = pl.multiple_of(block * 162 // 8 * 8, 8)
            left = total[pl.ds(start, 168), 0:128]
            right = jnp.concatenate(
                [
                    total[pl.ds(start, 88), 128:192],
                    total[pl.ds(pl.multiple_of(start + 80, 8), 88), 128:192],
                ],
                axis=1,
            )
            if own:
                keep[m * 256 : m * 256 + 168, :] = left
                keep[m * 256 + 168 : m * 256 + 256, :] = right
            else:
                send[m * 256 : m * 256 + 168, :] = left.astype(BF)
                send[m * 256 + 168 : m * 256 + 256, :] = right.astype(BF)


def scatter_shift(first, second, axis):
    step = {2: 16, 0: 4, 1: 1}[axis]
    at = row_ids() // step % 4
    down = pltpu.roll(second, step, 0)
    out = pltpu.roll(second, 64 - 3 * step, 0)
    return first + jnp.where(at == 0, 0.0, down), jnp.where(at == 0, out, 0.0)


def forward_kernel(
    lrules, lcodes, rrules, rcodes, split, weight,
    local, to_x, to_y, to_xy, regions, sums, pack,
):
    for shift in range(8):
        acc = None
        for index, tap in enumerate(TAPS):
            if tap_shift(tap) == shift:
                part = jnp.dot(
                    split[tap_parity(tap)],
                    weight[index * 192 : (index + 1) * 192, :],
                    preferred_element_type=F32,
                )
                acc = part if acc is None else acc + part
        for slot in range(3):
            regions[slot * 8 + shift] = acc[slot * 64 : slot * 64 + 64]
    for slot in range(3):
        for bit, axis in ((1, 0), (2, 1), (4, 2)):
            for other in range(8):
                if other & bit:
                    continue
                inner, outer = scatter_shift(
                    regions[slot * 8 + other], regions[slot * 8 + other + bit], axis
                )
                regions[slot * 8 + other] = inner
                regions[slot * 8 + other + bit] = outer
    for entry in range(16):
        sums[entry] = jnp.zeros((64, 192), F32)
    for e in range(12):
        at = jnp.minimum(lrules[0, 0, 0, e], 2) * 8 + lcodes[0, 0, e]
        sums[lrules[0, 0, 1, e]] += regions[at]
    for m in range(3):
        for e in range(3):
            at = jnp.minimum(rrules[0, 0, 0, m, e], 2) * 8 + rcodes[0, 0, m, e]
            sums[(m + 1) * 4 + rrules[0, 0, 1, m, e]] += regions[at]
    for t in range(3):
        local[t] = sums[t]
        for r in range(4):
            pack[r * 4 : r * 4 + 4, :] = sums[4 + t, r * 16 : r * 16 + 4, :]
        to_x[t] = pack[...].astype(BF)
        for group, ref in ((8, to_y), (12, to_xy)):
            for r in range(4):
                for p in range(4):
                    pack[r * 4 + p : r * 4 + p + 1, :] = sums[
                        group + t, r * 16 + p * 4 : r * 16 + p * 4 + 1, :
                    ]
            ref[t] = pack[...].astype(BF)


def output_kernel(valid, local, got_x, got_y, got_xy, out, acc, low, high):
    for t in range(3):
        acc[...] = local[t]
        from_x = got_x[t].astype(F32)
        from_y = got_y[t].astype(F32) + got_xy[t].astype(F32)
        for r in range(4):
            acc[r * 16 : r * 16 + 4, :] += from_x[r * 4 : r * 4 + 4]
        for row in range(16):
            acc[row * 4 : row * 4 + 1, :] += from_y[row : row + 1]
        live = valid[0, 0, t].astype(F32)
        for r in range(4):
            rows = acc[r * 16 : r * 16 + 16, :] * live
            put = pl.ds(r, 16, stride=4)
            low[put, :] = rows[:, 0:128]
            high[put, :] = jnp.concatenate([rows[:, 128:192], rows[:, 128:192]], axis=1)
        out[0, 0, t, :, 0:128] = low[...].astype(BF)
        out[0, 0, t, :, 128:192] = high[:, 0:64].astype(BF)


def features_kernel(valid, shifts, weight, out, low, high):
    for par in range(8):
        acc = None
        for index, tap in enumerate(TAPS):
            if tap_parity(tap) == par:
                part = lax.dot_general(
                    shifts[tap_shift(tap)],
                    weight[index * 192 : (index + 1) * 192, :],
                    (((1,), (1,)), ((), ())),
                    preferred_element_type=F32,
                )
                acc = part if acc is None else acc + part
        a, b, c = par // 4, par // 2 % 2, par % 2
        for slot in range(3):
            live = valid[0, 0, slot].astype(F32)
            for k in range(4):
                rows = acc[slot * 64 + k * 16 : slot * 64 + k * 16 + 16] * live
                put = pl.ds(slot * 512 + a * 256 + b * 8 + 2 * k + c, 16, stride=16)
                low[put, :] = rows[:, 0:128]
                high[put, :] = jnp.concatenate([rows[:, 128:192], rows[:, 128:192]], axis=1)
    for slot in range(3):
        for x in range(8):
            start = slot * 512 + ((x % 2) * 4 + x // 2) * 64
            rows = slice(x * 64, x * 64 + 64)
            out[0, 0, slot, rows, 0:128] = low[start : start + 64, :].astype(BF)
            out[0, 0, slot, rows, 128:192] = high[start : start + 64, 0:64].astype(BF)


def share_kernel(mine, other, out, rows):
    full = mine[...] + other[...]
    rows[:, 0:128] = full[0:168]
    rows[0:88, 128:192] = full[168:256, 0:64]
    rows[88:168, 128:192] = full[176:256, 64:128]
    offset = lax.axis_index("gx") % 4 * 2
    for case in range(4):
        @pl.when(offset == case * 2)
        def _(case=case):
            out[...] = rows[case * 2 : case * 2 + 162, :]


def swap(value, axis, size, bits):
    return lax.ppermute(value, axis, [(i, i ^ bits) for i in range(size)])


def lower(value, size_x, size_y, step_x, step_y, sign):
    route = []
    for i in range(size_x):
        for j in range(size_y):
            to_i, to_j = i + sign * step_x, j + sign * step_y
            if 0 <= to_i < size_x and 0 <= to_j < size_y:
                route.append((i * size_y + j, to_i * size_y + to_j))
    return lax.ppermute(value, ("gx", "gy"), route)


def split_sum_kernel(count, mine, *refs):
    got, first, rest = refs[:count], refs[count], refs[count + 1 :]
    size = first.shape[0]
    for d in range(4):
        rows = slice(d * size, d * size + size)
        full = mine[rows, :]
        for ref in got:
            full = full + ref[rows, :].astype(F32)
        if d == 0:
            first[...] = full
        else:
            rest[d - 1][...] = full.astype(BF)


def split_sum(mine, got, name, limit):
    size = mine.shape[0] // 4
    outs = (jax.ShapeDtypeStruct((size, 128), F32),) + (jax.ShapeDtypeStruct((size, 128), BF),) * 3
    args = (mine, *got)
    kernel = functools.partial(split_sum_kernel, len(got))
    first, *rest = call(kernel, outs, args, (VM,) * len(args), [], 0, name, limit)
    return first, rest


def together(*values):
    return lax.optimization_barrier(values)


def shards(
    features, weight, cotangent, valid, local_rules, local_codes, remote_rules, remote_codes
):
    size_x, size_y = lax.axis_size("gx"), lax.axis_size("gy")
    rules = (local_rules, local_codes, remote_rules, remote_codes)
    cot_x = lower(cotangent, size_x, size_y, 1, 0, -1)
    cot_y = lower(cotangent, size_x, size_y, 0, 1, -1)
    cot_xy = lower(cotangent, size_x, size_y, 1, 1, -1)
    shape = jax.ShapeDtypeStruct
    flops = 2 * 27 * 192**3
    split = call(
        split_kernel,
        shape((8, 192, 192), BF),
        (valid, features),
        (SM, VM),
        [pltpu.VMEM((1536, 128), F32)] * 2,
        0,
        "split",
        8,
    )
    keep, send, shifts = call(
        weight_kernel,
        (shape((4096, 128), F32), shape((4096, 128), BF), shape((8, 192, 192), BF)),
        (*rules, split, cotangent, cot_x, cot_y, cot_xy),
        (SM,) * 4 + (VM,) * 5,
        [pltpu.VMEM((16, 64, 192), F32), pltpu.VMEM((32, 64, 192), F32)]
        + [pltpu.VMEM((64, 128), F32)] * 2
        + [pltpu.VMEM((5184, 192), F32)],
        flops,
        "weight_side",
        18,
    )
    first, rest = split_sum(keep, [swap(send, "gx", 32, 1)], "sum_core", 8)
    first, rest, split, shifts = together(first, rest, split, shifts)
    arrived = [swap(part, "gx", 32, 8 * d) for d, part in zip((1, 2, 3), rest)]
    local, to_x, to_y, to_xy = call(
        forward_kernel,
        (shape((3, 64, 192), F32),) + (shape((3, 16, 192), BF),) * 3,
        (*rules, split, weight),
        (SM,) * 4 + (VM,) * 2,
        [pltpu.VMEM((24, 64, 192), F32), pltpu.VMEM((16, 64, 192), F32), pltpu.VMEM((16, 192), F32)],
        flops,
        "forward",
        12,
    )
    got_x = lower(to_x, size_x, size_y, 1, 0, 1)
    got_y = lower(to_y, size_x, size_y, 0, 1, 1)
    got_xy = lower(to_xy, size_x, size_y, 1, 1, 1)
    features_grad = call(
        features_kernel,
        shape((1, 1, 3, 512, 192), BF),
        (valid, shifts, weight),
        (SM, VM, VM),
        [pltpu.VMEM((1536, 128), F32)] * 2,
        flops,
        "features_side",
        12,
    )
    arrived, features_grad = together(arrived, features_grad)
    first, rest = split_sum(first, arrived, "sum_y", 4)
    first, rest, got_x, got_y, got_xy = together(first, rest, got_x, got_y, got_xy)
    arrived = [swap(part, "gx", 32, 2 * d) for d, part in zip((1, 2, 3), rest)]
    output = call(
        output_kernel,
        shape((1, 1, 3, 64, 192), BF),
        (valid, local, got_x, got_y, got_xy),
        (SM,) + (VM,) * 4,
        [pltpu.VMEM((64, 192), F32)] + [pltpu.VMEM((64, 128), F32)] * 2,
        0,
        "output",
    )
    arrived, output = together(arrived, output)
    part = first + arrived[0].astype(F32) + arrived[1].astype(F32) + arrived[2].astype(F32)
    got = [swap(part, "gy", 8, d) for d in (1, 2, 3)]
    mine = (part + got[0]) + (got[1] + got[2])
    other = swap(mine, "gy", 8, 4)
    weight_share = call(
        share_kernel,
        shape((162, 192), F32),
        (mine, other),
        (VM, VM),
        [pltpu.VMEM((168, 192), F32)],
        0,
        "share",
        2,
    )
    return output, features_grad, weight_share


def solution(mesh):
    return jax.shard_map(
        shards,
        mesh=mesh,
        in_specs=(
            P("gx", "gy", None, None, None),
            P(),
            P("gx", "gy", None, None, None),
            P("gx", "gy", None),
            P("gx", "gy", None, None),
            P("gx", "gy", None),
            P("gx", "gy", None, None, None),
            P("gx", "gy", None, None),
        ),
        out_specs=(P("gx", "gy", None, None, None), P("gx", "gy", None, None, None), P("gx", None)),
        check_vma=False,
    )
```

```python
import functools

import jax
import jax.numpy as jnp
from jax import lax
from jax.experimental import pallas as pl
from jax.experimental.pallas import tpu as pltpu
from jax.sharding import PartitionSpec as P

INTERPRET = False
BF = jnp.bfloat16
F32 = jnp.float32
VM = pltpu.MemorySpace.VMEM
HB = pltpu.MemorySpace.HBM
TABLES = ((1, 1, 2, 12), (1, 1, 12), (1, 1, 3, 2, 3), (1, 3, 1, 3))
FLAGS = ((1, 1, 3),)

PARITY = (1, 0, 1)
SHIFT = (1, 0, 0)
TAPS = [(e, f, g) for e in range(3) for f in range(3) for g in range(3)]


def tap_parity(tap):
    return PARITY[tap[0]] * 4 + PARITY[tap[1]] * 2 + PARITY[tap[2]]


def tap_shift(tap):
    return SHIFT[tap[0]] + 2 * SHIFT[tap[1]] + 4 * SHIFT[tap[2]]


def call(kernel, outs, args, spaces, scratch, flops, name, limit=4):
    nbytes = sum(a.size * a.dtype.itemsize for a in args)
    if not INTERPRET:
        args = [
            pltpu.with_memory_space_constraint(a, HB) if s == HB else a
            for a, s in zip(args, spaces)
        ]
    return pl.pallas_call(
        kernel,
        out_shape=outs,
        in_specs=[pl.BlockSpec(memory_space=s) for s in spaces],
        out_specs=jax.tree.map(lambda _: pl.BlockSpec(memory_space=VM), outs),
        scratch_shapes=scratch,
        compiler_params=pltpu.CompilerParams(vmem_limit_bytes=limit << 20),
        cost_estimate=pl.CostEstimate(flops=flops, bytes_accessed=nbytes, transcendentals=0),
        interpret=INTERPRET,
        name=name,
    )(*args)


def scalars(shapes):
    return [pltpu.SMEM(shape, jnp.int32) for shape in shapes] + [
        pltpu.SemaphoreType.DMA((len(shapes),))
    ]


def fetch(sources, targets, sems):
    copies = [
        pltpu.make_async_copy(source, target, sems.at[n])
        for n, (source, target) in enumerate(zip(sources, targets))
    ]
    for copy in copies:
        copy.start()
    return copies


def parity_order():
    row = lax.broadcasted_iota(jnp.int32, (512, 512), 0)
    voxel = lax.broadcasted_iota(jnp.int32, (512, 512), 1)
    par, r, p, q = row >> 6, row >> 4 & 3, row >> 2 & 3, row & 3
    x = 2 * p + (par >> 2)
    y = 2 * q + (par >> 1 & 1)
    z = 2 * r + (par & 1)
    return jnp.where(voxel == x * 64 + y * 8 + z, 1.0, 0.0).astype(BF)


def split_kernel(valid_in, feat, out, valid, sems):
    copies = fetch((valid_in,), (valid,), sems)
    order = parity_order()
    for copy in copies:
        copy.wait()
    for slot in range(3):
        rows = lax.dot_general(
            order, feat[0, 0, slot], (((1,), (1,)), ((), ())), preferred_element_type=F32
        )
        rows = (rows * valid[0, 0, slot].astype(F32)).astype(BF)
        for par in range(8):
            out[par, slot * 64 : slot * 64 + 64, :] = rows[par * 64 : par * 64 + 64]


def row_ids():
    return lax.broadcasted_iota(jnp.int32, (64, 192), 0)


def gather_shift(first, second, axis):
    if axis == 2:
        return jnp.concatenate([first[16:], second[:16]], axis=0)
    step = 4 if axis == 0 else 1
    at = row_ids() // step % 4
    up = pltpu.roll(first, 64 - step, 0)
    wrap = pltpu.roll(second, 3 * step, 0)
    return jnp.where(at == 3, wrap, up)


def to_cube_order(cube, low, high):
    low[...] = cube[:, :128]
    high[:, 0:64] = cube[:, 128:]
    parts = []
    for r in range(4):
        take = pl.ds(r, 16, stride=4)
        parts.append(jnp.concatenate([low[take, :], high[take, :][:, 0:64]], axis=1))
    return jnp.concatenate(parts, axis=0)


def weight_kernel(
    lrules_in, lcodes_in, rrules_in, rcodes_in, split, cot, cot_x, cot_y, cot_xy,
    keep, send, shifts, cubes, grads, low, high, total, lrules, lcodes, rrules, rcodes, sems,
):
    copies = fetch(
        (lrules_in, lcodes_in, rrules_in, rcodes_in), (lrules, lcodes, rrules, rcodes), sems
    )
    zero = jnp.zeros((64, 192), F32)
    for group, ref in enumerate((cot, cot_x, cot_y, cot_xy)):
        for slot in range(3):
            rows = ref[0, 0, slot].astype(F32)
            cubes[group * 4 + slot] = to_cube_order(rows, low, high)
        cubes[group * 4 + 3] = zero
    for entry in range(32):
        grads[entry] = zero
    for copy in copies:
        copy.wait()
    for e in range(12):
        at = lrules[0, 0, 0, e] * 8 + lcodes[0, 0, e]
        grads[at] += cubes[lrules[0, 0, 1, e]]
    for m in range(3):
        for e in range(3):
            at = rrules[0, 0, m, 0, e] * 8 + rcodes[0, m, 0, e]
            grads[at] += cubes[(m + 1) * 4 + rrules[0, 0, m, 1, e]]
    for slot in range(3):
        level = {}
        for u in range(2):
            for v in range(2):
                first = grads[slot * 8 + u + 2 * v]
                second = grads[slot * 8 + u + 2 * v + 4]
                level[u, v, 0] = first
                level[u, v, 1] = gather_shift(first, second, 2)
        after = {}
        for v in range(2):
            for w in range(2):
                after[0, v, w] = level[0, v, w]
                after[1, v, w] = gather_shift(level[0, v, w], level[1, v, w], 0)
        for u in range(2):
            for w in range(2):
                rows = slice(slot * 64, slot * 64 + 64)
                shifts[u + 4 * w, rows, :] = after[u, 0, w].astype(BF)
                shifts[u + 2 + 4 * w, rows, :] = gather_shift(
                    after[u, 0, w], after[u, 1, w], 1
                ).astype(BF)
    for index, tap in enumerate(TAPS):
        total[index * 192 : (index + 1) * 192, :] = lax.dot_general(
            split[tap_parity(tap)],
            shifts[tap_shift(tap)],
            (((0,), (0,)), ((), ())),
            preferred_element_type=F32,
        )
    here = lax.axis_index("gx")
    core = here % 2
    for m in range(16):
        other = m % 4 * 4 + m // 4
        for own in range(2):
            keeper = core if own else 1 - core
            block = ((here // 2) ^ jnp.where(keeper == 0, m, other)) * 2 + keeper
            start = pl.multiple_of(block * 162 // 8 * 8, 8)
            left = total[pl.ds(start, 168), 0:128]
            right = jnp.concatenate(
                [
                    total[pl.ds(start, 88), 128:192],
                    total[pl.ds(pl.multiple_of(start + 80, 8), 88), 128:192],
                ],
                axis=1,
            )
            if own:
                keep[m * 256 : m * 256 + 168, :] = left
                keep[m * 256 + 168 : m * 256 + 256, :] = right
            else:
                send[m * 256 : m * 256 + 168, :] = left.astype(BF)
                send[m * 256 + 168 : m * 256 + 256, :] = right.astype(BF)


def scatter_shift(first, second, axis):
    step = {2: 16, 0: 4, 1: 1}[axis]
    at = row_ids() // step % 4
    down = pltpu.roll(second, step, 0)
    out = pltpu.roll(second, 64 - 3 * step, 0)
    return first + jnp.where(at == 0, 0.0, down), jnp.where(at == 0, out, 0.0)


def forward_kernel(
    lrules_in, lcodes_in, rrules_in, rcodes_in, split, weight,
    local, to_x, to_y, to_xy, regions, sums, pack, lrules, lcodes, rrules, rcodes, sems,
):
    copies = fetch(
        (lrules_in, lcodes_in, rrules_in, rcodes_in), (lrules, lcodes, rrules, rcodes), sems
    )
    for shift in range(8):
        acc = None
        for index, tap in enumerate(TAPS):
            if tap_shift(tap) == shift:
                part = lax.dot_general(
                    split[tap_parity(tap)],
                    weight[:, index * 192 : (index + 1) * 192],
                    (((1,), (1,)), ((), ())),
                    preferred_element_type=F32,
                )
                acc = part if acc is None else acc + part
        for slot in range(3):
            regions[slot * 8 + shift] = acc[slot * 64 : slot * 64 + 64]
    for slot in range(3):
        for bit, axis in ((1, 0), (2, 1), (4, 2)):
            for other in range(8):
                if other & bit:
                    continue
                inner, outer = scatter_shift(
                    regions[slot * 8 + other], regions[slot * 8 + other + bit], axis
                )
                regions[slot * 8 + other] = inner
                regions[slot * 8 + other + bit] = outer
    for entry in range(16):
        sums[entry] = jnp.zeros((64, 192), F32)
    for copy in copies:
        copy.wait()
    for e in range(12):
        at = jnp.minimum(lrules[0, 0, 0, e], 2) * 8 + lcodes[0, 0, e]
        sums[lrules[0, 0, 1, e]] += regions[at]
    for m in range(3):
        for e in range(3):
            at = jnp.minimum(rrules[0, 0, m, 0, e], 2) * 8 + rcodes[0, m, 0, e]
            sums[(m + 1) * 4 + rrules[0, 0, m, 1, e]] += regions[at]
    for t in range(3):
        local[t] = sums[t]
        for r in range(4):
            pack[r * 4 : r * 4 + 4, :] = sums[4 + t, r * 16 : r * 16 + 4, :]
        to_x[t] = pack[...].astype(BF)
        for group, ref in ((8, to_y), (12, to_xy)):
            for r in range(4):
                for p in range(4):
                    pack[r * 4 + p : r * 4 + p + 1, :] = sums[
                        group + t, r * 16 + p * 4 : r * 16 + p * 4 + 1, :
                    ]
            ref[t] = pack[...].astype(BF)


def output_kernel(valid_in, local, got_x, got_y, got_xy, out, acc, low, high, valid, sems):
    for copy in fetch((valid_in,), (valid,), sems):
        copy.wait()
    for t in range(3):
        acc[...] = local[t]
        from_x = got_x[t].astype(F32)
        from_y = got_y[t].astype(F32) + got_xy[t].astype(F32)
        for r in range(4):
            acc[r * 16 : r * 16 + 4, :] += from_x[r * 4 : r * 4 + 4]
        for row in range(16):
            acc[row * 4 : row * 4 + 1, :] += from_y[row : row + 1]
        live = valid[0, 0, t].astype(F32)
        for r in range(4):
            rows = acc[r * 16 : r * 16 + 16, :] * live
            put = pl.ds(r, 16, stride=4)
            low[put, :] = rows[:, 0:128]
            high[put, :] = jnp.concatenate([rows[:, 128:192], rows[:, 128:192]], axis=1)
        out[0, 0, t, :, 0:128] = low[...].astype(BF)
        out[0, 0, t, :, 128:192] = high[:, 0:64].astype(BF)


def features_kernel(valid_in, shifts, weight, out, cubes, valid, sems):
    for copy in fetch((valid_in,), (valid,), sems):
        copy.wait()
    for par in range(8):
        acc = None
        for index, tap in enumerate(TAPS):
            if tap_parity(tap) == par:
                part = jnp.dot(
                    shifts[tap_shift(tap)],
                    weight[:, index * 192 : (index + 1) * 192],
                    preferred_element_type=F32,
                )
                acc = part if acc is None else acc + part
        for slot in range(3):
            live = valid[0, 0, slot].astype(F32)
            rows = acc[slot * 64 : slot * 64 + 64] * live
            cubes[slot, par * 64 : par * 64 + 64, :] = rows.astype(BF)
    order = parity_order()
    for slot in range(3):
        out[0, 0, slot] = lax.dot_general(
            cubes[slot], order, (((0,), (0,)), ((), ())), preferred_element_type=F32
        ).astype(BF)


def share_kernel(mine, other, out, rows):
    full = mine[...].astype(F32) + other[...].astype(F32)
    rows[:, 0:128] = full[0:168]
    rows[0:88, 128:192] = full[168:256, 0:64]
    rows[88:168, 128:192] = full[176:256, 64:128]
    offset = lax.axis_index("gx") % 4 * 2
    for case in range(4):
        @pl.when(offset == case * 2)
        def _(case=case):
            out[...] = rows[case * 2 : case * 2 + 162, :]


def swap(value, axis, size, bits):
    return lax.ppermute(value, axis, [(i, i ^ bits) for i in range(size)])


def lower(value, size_x, size_y, step_x, step_y, sign):
    route = []
    for i in range(size_x):
        for j in range(size_y):
            to_i, to_j = i + sign * step_x, j + sign * step_y
            if 0 <= to_i < size_x and 0 <= to_j < size_y:
                route.append((i * size_y + j, to_i * size_y + to_j))
    return lax.ppermute(value, ("gx", "gy"), route)


def split_sum_kernel(count, mine, *refs):
    got, first, rest = refs[:count], refs[count], refs[count + 1 :]
    size = first.shape[0]
    for d in range(4):
        rows = slice(d * size, d * size + size)
        full = mine[rows, :]
        for ref in got:
            full = full + ref[rows, :].astype(F32)
        if d == 0:
            first[...] = full
        else:
            rest[d - 1][...] = full.astype(BF)


def split_sum(mine, got, name, limit):
    size = mine.shape[0] // 4
    outs = (jax.ShapeDtypeStruct((size, 128), F32),) + (jax.ShapeDtypeStruct((size, 128), BF),) * 3
    args = (mine, *got)
    kernel = functools.partial(split_sum_kernel, len(got))
    first, *rest = call(kernel, outs, args, (VM,) * len(args), [], 0, name, limit)
    return first, rest


def sum_kernel(first, one, two, three, out):
    total = first[...].astype(F32) + one[...].astype(F32)
    out[...] = (total + (two[...].astype(F32) + three[...].astype(F32))).astype(BF)


def sum_of(values, name):
    return call(
        sum_kernel, jax.ShapeDtypeStruct((256, 128), BF), values, (VM,) * 4, [], 0, name, 2
    )


def turns(parts, first_bits, second_bits):
    got = {}
    for d in (2, 3, 1):
        route = [(i, i ^ ((second_bits if i % 2 else first_bits) * d)) for i in range(32)]
        got[d] = lax.ppermute(parts[d - 1], "gx", route)
    return [got[1], got[2], got[3]]


def together(*values):
    return lax.optimization_barrier(values)


def shards(
    features, weight, cotangent, valid, local_rules, local_codes, remote_rules, remote_codes
):
    size_x, size_y = lax.axis_size("gx"), lax.axis_size("gy")
    rules = (
        local_rules,
        local_codes,
        jnp.transpose(remote_rules, (0, 1, 3, 2, 4)),
        jnp.transpose(remote_codes, (0, 2, 1, 3)),
    )
    weight = weight.T
    features = jnp.swapaxes(features, 3, 4)
    cotangent = cotangent * valid.astype(BF)[..., None, None]
    cot_x = lower(cotangent, size_x, size_y, 1, 0, -1)
    cot_y = lower(cotangent, size_x, size_y, 0, 1, -1)
    cot_xy = lower(cotangent, size_x, size_y, 1, 1, -1)
    shape = jax.ShapeDtypeStruct
    flops = 2 * 27 * 192**3
    split = call(
        split_kernel, shape((8, 192, 192), BF), (valid, features), (HB, VM), scalars(FLAGS), 0, "split", 6
    )
    keep, send, shifts = call(
        weight_kernel,
        (shape((4096, 128), F32), shape((4096, 128), BF), shape((8, 192, 192), BF)),
        (*rules, split, cotangent, cot_x, cot_y, cot_xy),
        (HB,) * 4 + (VM,) * 5,
        [pltpu.VMEM((16, 64, 192), F32), pltpu.VMEM((32, 64, 192), F32)]
        + [pltpu.VMEM((64, 128), F32)] * 2
        + [pltpu.VMEM((5184, 192), F32)]
        + scalars(TABLES),
        flops,
        "weight_side",
        18,
    )
    send, split, weight = together(send, split, weight)
    arrived = swap(send, "gx", 32, 1)
    local, to_x, to_y, to_xy = call(
        forward_kernel,
        (shape((3, 64, 192), F32),) + (shape((3, 16, 192), BF),) * 3,
        (*rules, split, weight),
        (HB,) * 4 + (VM,) * 2,
        [pltpu.VMEM((24, 64, 192), F32), pltpu.VMEM((16, 64, 192), F32), pltpu.VMEM((16, 192), F32)]
        + scalars(TABLES),
        flops,
        "forward",
        12,
    )
    arrived, local, to_x, to_y, to_xy = together(arrived, local, to_x, to_y, to_xy)
    first, rest = split_sum(keep, [arrived], "sum_core", 8)
    rest, shifts = together(rest, shifts)
    arrived = turns(rest, 8, 2)
    features_grad = call(
        features_kernel,
        shape((1, 1, 3, 192, 512), BF),
        (valid, shifts, weight),
        (HB, VM, VM),
        [pltpu.VMEM((3, 512, 192), BF)] + scalars(FLAGS),
        flops,
        "features_side",
        12,
    )
    features_grad, to_x, to_y, to_xy = together(features_grad, to_x, to_y, to_xy)
    got_x = lower(to_x, size_x, size_y, 1, 0, 1)
    got_y = lower(to_y, size_x, size_y, 0, 1, 1)
    got_xy = lower(to_xy, size_x, size_y, 1, 1, 1)
    arrived, features_grad = together(arrived, features_grad)
    first, rest = split_sum(first, arrived, "sum_one", 4)
    rest, got_x, got_y, got_xy = together(rest, got_x, got_y, got_xy)
    arrived = turns(rest, 2, 8)
    output = call(
        output_kernel,
        shape((1, 1, 3, 64, 192), BF),
        (valid, local, got_x, got_y, got_xy),
        (HB,) + (VM,) * 4,
        [pltpu.VMEM((64, 192), F32)] + [pltpu.VMEM((64, 128), F32)] * 2 + scalars(FLAGS),
        0,
        "output",
    )
    arrived, output = together(arrived, output)
    part = sum_of((first, *arrived), "sum_two")
    part = sum_of((part, *(swap(part, "gy", 8, d) for d in (1, 2, 3))), "sum_x")
    weight_share = call(
        share_kernel,
        shape((162, 192), F32),
        (part, swap(part, "gy", 8, 4)),
        (VM, VM),
        [pltpu.VMEM((168, 192), F32)],
        0,
        "share",
        2,
    )
    features_grad = jnp.swapaxes(features_grad, 3, 4)
    return output, features_grad, weight_share


def solution(mesh):
    return jax.shard_map(
        shards,
        mesh=mesh,
        in_specs=(
            P("gx", "gy", None, None, None),
            P(),
            P("gx", "gy", None, None, None),
            P("gx", "gy", None),
            P("gx", "gy", None, None),
            P("gx", "gy", None),
            P("gx", "gy", None, None, None),
            P("gx", "gy", None, None),
        ),
        out_specs=(P("gx", "gy", None, None, None), P("gx", "gy", None, None, None), P("gx", None)),
        check_vma=False,
    )
```

```python
import functools

import jax
import jax.numpy as jnp
from jax import lax
from jax.experimental import pallas as pl
from jax.experimental.pallas import tpu as pltpu
from jax.sharding import PartitionSpec as P

INTERPRET = False
BF = jnp.bfloat16
F32 = jnp.float32
VM = pltpu.MemorySpace.VMEM
HB = pltpu.MemorySpace.HBM
TABLES = ((1, 1, 2, 12), (1, 1, 12), (1, 1, 3, 2, 3), (1, 3, 1, 3))
FLAGS = ((1, 1, 3),)

PARITY = (1, 0, 1)
SHIFT = (1, 0, 0)
TAPS = [(e, f, g) for e in range(3) for f in range(3) for g in range(3)]


def tap_parity(tap):
    return PARITY[tap[0]] * 4 + PARITY[tap[1]] * 2 + PARITY[tap[2]]


def tap_shift(tap):
    return SHIFT[tap[0]] + 2 * SHIFT[tap[1]] + 4 * SHIFT[tap[2]]


def call(kernel, outs, args, spaces, scratch, flops, name, limit=4):
    nbytes = sum(a.size * a.dtype.itemsize for a in args)
    if not INTERPRET:
        args = [
            pltpu.with_memory_space_constraint(a, HB) if s == HB else a
            for a, s in zip(args, spaces)
        ]
    return pl.pallas_call(
        kernel,
        out_shape=outs,
        in_specs=[pl.BlockSpec(memory_space=s) for s in spaces],
        out_specs=jax.tree.map(lambda _: pl.BlockSpec(memory_space=VM), outs),
        scratch_shapes=scratch,
        compiler_params=pltpu.CompilerParams(vmem_limit_bytes=limit << 20),
        cost_estimate=pl.CostEstimate(flops=flops, bytes_accessed=nbytes, transcendentals=0),
        interpret=INTERPRET,
        name=name,
    )(*args)


def scalars(shapes):
    return [pltpu.SMEM(shape, jnp.int32) for shape in shapes] + [pltpu.SemaphoreType.DMA((8,))]


def fetch(sources, targets, sems):
    copies = [
        pltpu.make_async_copy(source, target, sems.at[n])
        for n, (source, target) in enumerate(zip(sources, targets))
    ]
    for copy in copies:
        copy.start()
    return copies


def parity_order():
    row = lax.broadcasted_iota(jnp.int32, (512, 512), 0)
    voxel = lax.broadcasted_iota(jnp.int32, (512, 512), 1)
    par, r, p, q = row >> 6, row >> 4 & 3, row >> 2 & 3, row & 3
    x = 2 * p + (par >> 2)
    y = 2 * q + (par >> 1 & 1)
    z = 2 * r + (par & 1)
    return jnp.where(voxel == x * 64 + y * 8 + z, 1.0, 0.0).astype(BF)


def split_kernel(valid_in, feat_in, out, feat, valid, sems):
    copies = fetch((valid_in, feat_in), (valid, feat), sems)
    order = parity_order()
    for copy in copies:
        copy.wait()
    for slot in range(3):
        rows = lax.dot_general(
            order, feat[0, 0, slot], (((1,), (1,)), ((), ())), preferred_element_type=F32
        )
        rows = (rows * valid[0, 0, slot].astype(F32)).astype(BF)
        for par in range(8):
            out[par, slot * 64 : slot * 64 + 64, :] = rows[par * 64 : par * 64 + 64]


def mask_kernel(valid_in, cot_in, masked, face, cot, valid, sems):
    for copy in fetch((valid_in, cot_in), (valid, cot), sems):
        copy.wait()
    for slot in range(3):
        rows = cot[0, 0, slot].astype(F32) * valid[0, 0, slot].astype(F32)
        rows = rows.astype(BF)
        masked[slot] = rows
        face[slot] = rows[0:16]


def pack_kernel(masked, cot_x, out):
    for slot in range(3):
        rows = masked[slot].astype(F32)
        edge = cot_x[slot].astype(F32)[0:4]
        face = [rows[p * 16 : p * 16 + 4] for p in range(4)]
        out[slot] = jnp.concatenate(face + [edge, jnp.zeros((12, 192), F32)], axis=0).astype(BF)


def row_ids():
    return lax.broadcasted_iota(jnp.int32, (64, 192), 0)


def gather_shift(first, second, axis):
    if axis == 2:
        return jnp.concatenate([first[16:], second[:16]], axis=0)
    step = 4 if axis == 0 else 1
    at = row_ids() // step % 4
    up = pltpu.roll(first, 64 - step, 0)
    wrap = pltpu.roll(second, 3 * step, 0)
    return jnp.where(at == 3, wrap, up)


def to_cube_order(cube, low, high):
    low[...] = cube[:, :128]
    high[:, 0:64] = cube[:, 128:]
    parts = []
    for r in range(4):
        take = pl.ds(r, 16, stride=4)
        parts.append(jnp.concatenate([low[take, :], high[take, :][:, 0:64]], axis=1))
    return jnp.concatenate(parts, axis=0)


def weight_kernel(
    lrules_in, lcodes_in, rrules_in, rcodes_in, split, masked, cot_x, cot_y,
    keep, send, shifts, cubes, grads, low, high, total, lrules, lcodes, rrules, rcodes, sems,
):
    copies = fetch(
        (lrules_in, lcodes_in, rrules_in, rcodes_in), (lrules, lcodes, rrules, rcodes), sems
    )
    zero = jnp.zeros((64, 192), F32)
    for group in range(16):
        cubes[group] = zero
    for slot in range(3):
        cubes[slot] = to_cube_order(masked[slot].astype(F32), low, high)
        from_x = cot_x[slot].astype(F32)
        from_y = cot_y[slot].astype(F32)
        for r in range(4):
            for n in range(4):
                put = slice(r * 16 + n, r * 16 + n + 1)
                cubes[4 + slot, put, :] = from_x[n * 4 + r : n * 4 + r + 1]
                put = slice(r * 16 + n * 4, r * 16 + n * 4 + 1)
                cubes[8 + slot, put, :] = from_y[n * 4 + r : n * 4 + r + 1]
            put = slice(r * 16, r * 16 + 1)
            cubes[12 + slot, put, :] = from_y[16 + r : 17 + r]
    for entry in range(32):
        grads[entry] = zero
    for copy in copies:
        copy.wait()
    for e in range(12):
        at = lrules[0, 0, 0, e] * 8 + lcodes[0, 0, e]
        grads[at] += cubes[lrules[0, 0, 1, e]]
    for m in range(3):
        for e in range(3):
            at = rrules[0, 0, m, 0, e] * 8 + rcodes[0, m, 0, e]
            grads[at] += cubes[(m + 1) * 4 + rrules[0, 0, m, 1, e]]
    for slot in range(3):
        level = {}
        for u in range(2):
            for v in range(2):
                first = grads[slot * 8 + u + 2 * v]
                second = grads[slot * 8 + u + 2 * v + 4]
                level[u, v, 0] = first
                level[u, v, 1] = gather_shift(first, second, 2)
        after = {}
        for v in range(2):
            for w in range(2):
                after[0, v, w] = level[0, v, w]
                after[1, v, w] = gather_shift(level[0, v, w], level[1, v, w], 0)
        for u in range(2):
            for w in range(2):
                rows = slice(slot * 64, slot * 64 + 64)
                shifts[u + 4 * w, rows, :] = after[u, 0, w].astype(BF)
                shifts[u + 2 + 4 * w, rows, :] = gather_shift(
                    after[u, 0, w], after[u, 1, w], 1
                ).astype(BF)
    for index, tap in enumerate(TAPS):
        total[index * 192 : (index + 1) * 192, :] = lax.dot_general(
            split[tap_parity(tap)],
            shifts[tap_shift(tap)],
            (((0,), (0,)), ((), ())),
            preferred_element_type=F32,
        )
    here = lax.axis_index("gx")
    core = here % 2
    column = lax.axis_index("gy") % 4
    for m in range(16):
        y_step, z_step = m // 4, m % 4
        for own in range(2):
            keeper = core if own else 1 - core
            block = ((here // 2) ^ m) * 2 + keeper
            start = pl.multiple_of(block * 162 // 8 * 8, 8)
            left = total[pl.ds(start, 168), 0:128]
            right = jnp.concatenate(
                [
                    total[pl.ds(start, 88), 128:192],
                    total[pl.ds(pl.multiple_of(start + 80, 8), 88), 128:192],
                ],
                axis=1,
            )
            rows = jnp.concatenate([left, right], axis=0)
            for quarter in range(4):
                x_step = quarter ^ column
                first = jnp.where(keeper == 0, x_step, y_step)
                second = jnp.where(keeper == 0, y_step, x_step)
                at = pl.multiple_of(first * 1024 + second * 256 + z_step * 64, 64)
                part = rows[quarter * 64 : quarter * 64 + 64]
                if own:
                    keep[pl.ds(at, 64), :] = part
                else:
                    send[pl.ds(at, 64), :] = part.astype(BF)


def scatter_shift(first, second, axis):
    step = {2: 16, 0: 4, 1: 1}[axis]
    at = row_ids() // step % 4
    down = pltpu.roll(second, step, 0)
    out = pltpu.roll(second, 64 - 3 * step, 0)
    return first + jnp.where(at == 0, 0.0, down), jnp.where(at == 0, out, 0.0)


def forward_kernel(
    lrules_in, lcodes_in, rrules_in, rcodes_in, split, weight,
    local, to_x, to_y, regions, sums, pack, lrules, lcodes, rrules, rcodes, sems,
):
    copies = fetch(
        (lrules_in, lcodes_in, rrules_in, rcodes_in), (lrules, lcodes, rrules, rcodes), sems
    )
    for shift in range(8):
        acc = None
        for index, tap in enumerate(TAPS):
            if tap_shift(tap) == shift:
                part = lax.dot_general(
                    split[tap_parity(tap)],
                    weight[:, index * 192 : (index + 1) * 192],
                    (((1,), (1,)), ((), ())),
                    preferred_element_type=F32,
                )
                acc = part if acc is None else acc + part
        for slot in range(3):
            regions[slot * 8 + shift] = acc[slot * 64 : slot * 64 + 64]
    for slot in range(3):
        for bit, axis in ((1, 0), (2, 1), (4, 2)):
            for other in range(8):
                if other & bit:
                    continue
                inner, outer = scatter_shift(
                    regions[slot * 8 + other], regions[slot * 8 + other + bit], axis
                )
                regions[slot * 8 + other] = inner
                regions[slot * 8 + other + bit] = outer
    for entry in range(16):
        sums[entry] = jnp.zeros((64, 192), F32)
    for copy in copies:
        copy.wait()
    for e in range(12):
        at = jnp.minimum(lrules[0, 0, 0, e], 2) * 8 + lcodes[0, 0, e]
        sums[lrules[0, 0, 1, e]] += regions[at]
    for m in range(3):
        for e in range(3):
            at = jnp.minimum(rrules[0, 0, m, 0, e], 2) * 8 + rcodes[0, m, 0, e]
            sums[(m + 1) * 4 + rrules[0, 0, m, 1, e]] += regions[at]
    for t in range(3):
        local[t] = sums[t]
        pack[16:32, :] = jnp.zeros((16, 192), F32)
        for r in range(4):
            pack[r * 4 : r * 4 + 4, :] = sums[4 + t, r * 16 : r * 16 + 4, :]
            pack[16 + r : 17 + r, :] = sums[12 + t, r * 16 : r * 16 + 1, :]
            for p in range(4):
                to_y[t, r * 4 + p : r * 4 + p + 1, :] = sums[
                    8 + t, r * 16 + p * 4 : r * 16 + p * 4 + 1, :
                ]
        to_x[t] = pack[...].astype(BF)


def join_kernel(to_y, got_x, out, rows):
    for t in range(3):
        edge = got_x[t].astype(F32)
        rows[...] = to_y[t]
        for r in range(4):
            rows[r * 4 : r * 4 + 1, :] += edge[16 + r : 17 + r]
        out[t] = rows[...].astype(BF)


def output_kernel(valid_in, local, got_x, got_y, out, acc, low, high, valid, sems):
    for copy in fetch((valid_in,), (valid,), sems):
        copy.wait()
    for t in range(3):
        acc[...] = local[t]
        from_x = got_x[t].astype(F32)
        from_y = got_y[t].astype(F32)
        for r in range(4):
            acc[r * 16 : r * 16 + 4, :] += from_x[r * 4 : r * 4 + 4]
        for row in range(16):
            acc[row * 4 : row * 4 + 1, :] += from_y[row : row + 1]
        live = valid[0, 0, t].astype(F32)
        for r in range(4):
            rows = acc[r * 16 : r * 16 + 16, :] * live
            put = pl.ds(r, 16, stride=4)
            low[put, :] = rows[:, 0:128]
            high[put, :] = jnp.concatenate([rows[:, 128:192], rows[:, 128:192]], axis=1)
        out[0, 0, t, :, 0:128] = low[...].astype(BF)
        out[0, 0, t, :, 128:192] = high[:, 0:64].astype(BF)


def features_kernel(valid_in, shifts, weight, out, cubes, valid, sems):
    for copy in fetch((valid_in,), (valid,), sems):
        copy.wait()
    for par in range(8):
        acc = None
        for index, tap in enumerate(TAPS):
            if tap_parity(tap) == par:
                part = jnp.dot(
                    shifts[tap_shift(tap)],
                    weight[:, index * 192 : (index + 1) * 192],
                    preferred_element_type=F32,
                )
                acc = part if acc is None else acc + part
        for slot in range(3):
            live = valid[0, 0, slot].astype(F32)
            rows = acc[slot * 64 : slot * 64 + 64] * live
            cubes[slot, par * 64 : par * 64 + 64, :] = rows.astype(BF)
    order = parity_order()
    for slot in range(3):
        out[0, 0, slot] = lax.dot_general(
            cubes[slot], order, (((0,), (0,)), ((), ())), preferred_element_type=F32
        ).astype(BF)


def share_kernel(mine, one, two, three, out, full, rows):
    column = lax.axis_index("gy") % 4
    for d, ref in enumerate((mine, one, two, three)):
        full[pl.ds(pl.multiple_of((column ^ d) * 64, 64), 64), :] = ref[...]
    rows[:, 0:128] = full[0:168, :]
    rows[0:88, 128:192] = full[168:256, 0:64]
    rows[88:168, 128:192] = full[176:256, 64:128]
    offset = lax.axis_index("gx") % 4 * 2
    for case in range(4):
        @pl.when(offset == case * 2)
        def _(case=case):
            out[...] = rows[case * 2 : case * 2 + 162, :]


def swap(value, axis, size, bits):
    return lax.ppermute(value, axis, [(i, i ^ bits) for i in range(size)])


def step(value, axis, sign):
    size = lax.axis_size(axis)
    route = [(i, i + sign) for i in range(size) if 0 <= i + sign < size]
    return lax.ppermute(value, axis, route)


def split_sum_kernel(count, mine, *refs):
    got, first, rest = refs[:count], refs[count], refs[count + 1 :]
    size = first.shape[0]
    for d in range(4):
        rows = slice(d * size, d * size + size)
        full = mine[rows, :]
        for ref in got:
            full = full + ref[rows, :].astype(F32)
        if d == 0:
            first[...] = full
        else:
            rest[d - 1][...] = full.astype(BF)


def split_sum(mine, got, name, limit):
    size = mine.shape[0] // 4
    outs = (jax.ShapeDtypeStruct((size, 128), F32),) + (jax.ShapeDtypeStruct((size, 128), BF),) * 3
    args = (mine, *got)
    kernel = functools.partial(split_sum_kernel, len(got))
    first, *rest = call(kernel, outs, args, (VM,) * len(args), [], 0, name, limit)
    return first, rest


def sum_kernel(first, one, two, three, out):
    total = first[...] + one[...].astype(F32)
    out[...] = total + two[...].astype(F32) + three[...].astype(F32)


ALONG = {
    "x": lambda i, j, d: (i, j ^ d),
    "y": lambda i, j, d: (i ^ (8 * d), j),
    "z": lambda i, j, d: (i ^ (2 * d), j),
}


def turns(parts, axis_of_core):
    got = {}
    for d in (2, 3, 1):
        route = []
        for i in range(32):
            for j in range(8):
                to_i, to_j = ALONG[axis_of_core[i % 2]](i, j, d)
                route.append((i * 8 + j, to_i * 8 + to_j))
        got[d] = lax.ppermute(parts[d - 1], ("gx", "gy"), route)
    return [got[1], got[2], got[3]]


def together(*values):
    return lax.optimization_barrier(values)


def shards(
    features, weight, cotangent, valid, local_rules, local_codes, remote_rules, remote_codes
):
    rules = (
        local_rules,
        local_codes,
        jnp.transpose(remote_rules, (0, 1, 3, 2, 4)),
        jnp.transpose(remote_codes, (0, 2, 1, 3)),
    )
    weight = weight.T
    features = jnp.swapaxes(features, 3, 4)
    shape = jax.ShapeDtypeStruct
    flops = 2 * 27 * 192**3
    masked, face = call(
        mask_kernel,
        (shape((3, 64, 192), BF), shape((3, 16, 192), BF)),
        (valid, cotangent),
        (HB, HB),
        [pltpu.VMEM((1, 1, 3, 64, 192), BF)] + scalars(FLAGS),
        0,
        "mask",
        2,
    )
    cot_x = step(face, "gx", -1)
    split = call(
        split_kernel,
        shape((8, 192, 192), BF),
        (valid, features),
        (HB, HB),
        [pltpu.VMEM((1, 1, 3, 192, 512), BF)] + scalars(FLAGS),
        0,
        "split",
        6,
    )
    split, cot_x = together(split, cot_x)
    packed = call(
        pack_kernel, shape((3, 32, 192), BF), (masked, cot_x), (VM, VM), [], 0, "pack", 2,
    )
    cot_y = step(packed, "gy", -1)
    keep, send, shifts = call(
        weight_kernel,
        (shape((4096, 128), F32), shape((4096, 128), BF), shape((8, 192, 192), BF)),
        (*rules, split, masked, cot_x, cot_y),
        (HB,) * 4 + (VM,) * 4,
        [pltpu.VMEM((16, 64, 192), F32), pltpu.VMEM((32, 64, 192), F32)]
        + [pltpu.VMEM((64, 128), F32)] * 2
        + [pltpu.VMEM((5184, 192), F32)]
        + scalars(TABLES),
        flops,
        "weight_side",
        18,
    )
    send, split, weight = together(send, split, weight)
    arrived = swap(send, "gx", 32, 1)
    local, to_x, to_y = call(
        forward_kernel,
        (shape((3, 64, 192), F32), shape((3, 32, 192), BF), shape((3, 16, 192), F32)),
        (*rules, split, weight),
        (HB,) * 4 + (VM,) * 2,
        [pltpu.VMEM((24, 64, 192), F32), pltpu.VMEM((16, 64, 192), F32), pltpu.VMEM((32, 192), F32)]
        + scalars(TABLES),
        flops,
        "forward",
        12,
    )
    arrived, local, to_x, to_y = together(arrived, local, to_x, to_y)
    first, rest = split_sum(keep, [arrived], "sum_core", 8)
    rest, shifts = together(rest, shifts)
    arrived = turns(rest, "xy")
    features_grad = call(
        features_kernel,
        shape((1, 1, 3, 192, 512), BF),
        (valid, shifts, weight),
        (HB, VM, VM),
        [pltpu.VMEM((3, 512, 192), BF)] + scalars(FLAGS),
        flops,
        "features_side",
        12,
    )
    features_grad, to_x = together(features_grad, to_x)
    got_x = step(to_x, "gx", 1)
    arrived, features_grad = together(arrived, features_grad)
    first, rest = split_sum(first, arrived, "sum_one", 4)
    rest, got_x = together(rest, got_x)
    arrived = turns(rest, "yx")
    joined = call(
        join_kernel, shape((3, 16, 192), BF), (to_y, got_x), (VM, VM),
        [pltpu.VMEM((16, 192), F32)], 0, "join", 2,
    )
    got_y = step(joined, "gy", 1)
    arrived, joined = together(arrived, joined)
    first, rest = split_sum(first, arrived, "sum_two", 2)
    rest, got_y = together(rest, got_y)
    arrived = turns(rest, "zz")
    output = call(
        output_kernel,
        shape((1, 1, 3, 64, 192), BF),
        (valid, local, got_x, got_y),
        (HB,) + (VM,) * 3,
        [pltpu.VMEM((64, 192), F32)] + [pltpu.VMEM((64, 128), F32)] * 2 + scalars(FLAGS),
        0,
        "output",
    )
    arrived, output = together(arrived, output)
    part = call(
        sum_kernel, shape((64, 128), F32), (first, *arrived), (VM,) * 4, [], 0, "sum_z", 2
    )
    part = part + swap(part, "gy", 8, 4)
    weight_share = call(
        share_kernel,
        shape((162, 192), F32),
        (part, *(swap(part, "gy", 8, d) for d in (1, 2, 3))),
        (VM,) * 4,
        [pltpu.VMEM((256, 128), F32), pltpu.VMEM((168, 192), F32)],
        0,
        "share",
        2,
    )
    features_grad = jnp.swapaxes(features_grad, 3, 4)
    return output, features_grad, weight_share


def solution(mesh):
    return jax.shard_map(
        shards,
        mesh=mesh,
        in_specs=(
            P("gx", "gy", None, None, None),
            P(),
            P("gx", "gy", None, None, None),
            P("gx", "gy", None),
            P("gx", "gy", None, None),
            P("gx", "gy", None),
            P("gx", "gy", None, None, None),
            P("gx", "gy", None, None),
        ),
        out_specs=(P("gx", "gy", None, None, None), P("gx", "gy", None, None, None), P("gx", None)),
        check_vma=False,
    )
```

```python
import functools

import jax
import jax.numpy as jnp
from jax import lax
from jax.experimental import pallas as pl
from jax.experimental.pallas import tpu as pltpu
from jax.sharding import PartitionSpec as P


INTERPRET = False
BF = jnp.bfloat16
F32 = jnp.float32
VM = pltpu.MemorySpace.VMEM
HB = pltpu.MemorySpace.HBM
TABLES = ((1, 1, 2, 12), (1, 1, 12), (1, 1, 3, 2, 3), (1, 3, 1, 3))
FLAGS = ((1, 1, 3),)

PARITY = (1, 0, 1)
SHIFT = (1, 0, 0)
TAPS = [(e, f, g) for e in range(3) for f in range(3) for g in range(3)]


def tap_parity(tap):
    return PARITY[tap[0]] * 4 + PARITY[tap[1]] * 2 + PARITY[tap[2]]


def tap_shift(tap):
    return SHIFT[tap[0]] + 2 * SHIFT[tap[1]] + 4 * SHIFT[tap[2]]


def call(kernel, outs, args, spaces, scratch, flops, limit=4):
    nbytes = sum(a.size * a.dtype.itemsize for a in args)
    if not INTERPRET:
        args = [
            pltpu.with_memory_space_constraint(a, HB) if s == HB else a
            for a, s in zip(args, spaces)
        ]
    return pl.pallas_call(
        kernel,
        out_shape=outs,
        in_specs=[pl.BlockSpec(memory_space=s) for s in spaces],
        out_specs=jax.tree.map(lambda _: pl.BlockSpec(memory_space=VM), outs),
        scratch_shapes=scratch,
        compiler_params=pltpu.CompilerParams(vmem_limit_bytes=limit << 20),
        cost_estimate=pl.CostEstimate(flops=flops, bytes_accessed=nbytes, transcendentals=0),
        interpret=INTERPRET,
    )(*args)


def scalars(shapes):
    return [pltpu.SMEM(shape, jnp.int32) for shape in shapes] + [pltpu.SemaphoreType.DMA((8,))]


def fetch(sources, targets, sems):
    copies = [
        pltpu.make_async_copy(source, target, sems.at[n])
        for n, (source, target) in enumerate(zip(sources, targets))
    ]
    for copy in copies:
        copy.start()
    return copies


def parity_order():
    row = lax.broadcasted_iota(jnp.int32, (512, 512), 0)
    voxel = lax.broadcasted_iota(jnp.int32, (512, 512), 1)
    par, r, p, q = row >> 6, row >> 4 & 3, row >> 2 & 3, row & 3
    x = 2 * p + (par >> 2)
    y = 2 * q + (par >> 1 & 1)
    z = 2 * r + (par & 1)
    return jnp.where(voxel == x * 64 + y * 8 + z, 1.0, 0.0).astype(BF)


def split_kernel(valid_in, feat_in, out, feat, valid, sems):
    copies = fetch((valid_in, feat_in), (valid, feat), sems)
    order = parity_order()
    for copy in copies:
        copy.wait()
    for slot in range(3):
        rows = lax.dot_general(
            order, feat[0, 0, slot], (((1,), (1,)), ((), ())), preferred_element_type=F32
        )
        rows = (rows * valid[0, 0, slot].astype(F32)).astype(BF)
        for par in range(8):
            out[par, slot * 64 : slot * 64 + 64, :] = rows[par * 64 : par * 64 + 64]


def mask_kernel(valid_in, cot_in, masked, face, cot, valid, sems):
    for copy in fetch((valid_in, cot_in), (valid, cot), sems):
        copy.wait()
    for slot in range(3):
        rows = cot[0, 0, slot].astype(F32) * valid[0, 0, slot].astype(F32)
        rows = rows.astype(BF)
        masked[slot] = rows
        face[slot] = rows[0:16]


def pack_kernel(masked, cot_x, out):
    for slot in range(3):
        rows = masked[slot].astype(F32)
        edge = cot_x[slot].astype(F32)[0:4]
        face = [rows[p * 16 : p * 16 + 4] for p in range(4)]
        out[slot] = jnp.concatenate(face + [edge, jnp.zeros((12, 192), F32)], axis=0).astype(BF)


def row_ids():
    return lax.broadcasted_iota(jnp.int32, (64, 192), 0)


def gather_shift(first, second, axis):
    if axis == 2:
        return jnp.concatenate([first[16:], second[:16]], axis=0)
    step = 4 if axis == 0 else 1
    at = row_ids() // step % 4
    up = pltpu.roll(first, 64 - step, 0)
    wrap = pltpu.roll(second, 3 * step, 0)
    return jnp.where(at == 3, wrap, up)


def to_cube_order(cube, low, high):
    low[...] = cube[:, :128]
    high[:, 0:64] = cube[:, 128:]
    parts = []
    for r in range(4):
        take = pl.ds(r, 16, stride=4)
        parts.append(jnp.concatenate([low[take, :], high[take, :][:, 0:64]], axis=1))
    return jnp.concatenate(parts, axis=0)


def weight_kernel(
    lrules_in, lcodes_in, rrules_in, rcodes_in, split, masked, cot_x, cot_y,
    keep, send, shifts, cubes, grads, low, high, total, lrules, lcodes, rrules, rcodes, sems,
):
    copies = fetch(
        (lrules_in, lcodes_in, rrules_in, rcodes_in), (lrules, lcodes, rrules, rcodes), sems
    )
    zero = jnp.zeros((64, 192), F32)
    for group in range(16):
        cubes[group] = zero
    for slot in range(3):
        cubes[slot] = to_cube_order(masked[slot].astype(F32), low, high)
        from_x = cot_x[slot].astype(F32)
        from_y = cot_y[slot].astype(F32)
        for r in range(4):
            for n in range(4):
                put = slice(r * 16 + n, r * 16 + n + 1)
                cubes[4 + slot, put, :] = from_x[n * 4 + r : n * 4 + r + 1]
                put = slice(r * 16 + n * 4, r * 16 + n * 4 + 1)
                cubes[8 + slot, put, :] = from_y[n * 4 + r : n * 4 + r + 1]
            put = slice(r * 16, r * 16 + 1)
            cubes[12 + slot, put, :] = from_y[16 + r : 17 + r]
    for entry in range(32):
        grads[entry] = zero
    for copy in copies:
        copy.wait()
    for e in range(12):
        at = lrules[0, 0, 0, e] * 8 + lcodes[0, 0, e]
        grads[at] += cubes[lrules[0, 0, 1, e]]
    for m in range(3):
        for e in range(3):
            at = rrules[0, 0, m, 0, e] * 8 + rcodes[0, m, 0, e]
            grads[at] += cubes[(m + 1) * 4 + rrules[0, 0, m, 1, e]]
    for slot in range(3):
        level = {}
        for u in range(2):
            for v in range(2):
                first = grads[slot * 8 + u + 2 * v]
                second = grads[slot * 8 + u + 2 * v + 4]
                level[u, v, 0] = first
                level[u, v, 1] = gather_shift(first, second, 2)
        after = {}
        for v in range(2):
            for w in range(2):
                after[0, v, w] = level[0, v, w]
                after[1, v, w] = gather_shift(level[0, v, w], level[1, v, w], 0)
        for u in range(2):
            for w in range(2):
                rows = slice(slot * 64, slot * 64 + 64)
                shifts[u + 4 * w, rows, :] = after[u, 0, w].astype(BF)
                shifts[u + 2 + 4 * w, rows, :] = gather_shift(
                    after[u, 0, w], after[u, 1, w], 1
                ).astype(BF)
    for index, tap in enumerate(TAPS):
        total[index * 192 : (index + 1) * 192, :] = lax.dot_general(
            split[tap_parity(tap)],
            shifts[tap_shift(tap)],
            (((0,), (0,)), ((), ())),
            preferred_element_type=F32,
        )
    here = lax.axis_index("gx")
    core = here % 2
    for m in range(16):
        other = m % 4 * 4 + m // 4
        for own in range(2):
            keeper = core if own else 1 - core
            block = ((here // 2) ^ jnp.where(keeper == 0, m, other)) * 2 + keeper
            start = pl.multiple_of(block * 162 // 8 * 8, 8)
            left = total[pl.ds(start, 168), 0:128]
            right = jnp.concatenate(
                [
                    total[pl.ds(start, 88), 128:192],
                    total[pl.ds(pl.multiple_of(start + 80, 8), 88), 128:192],
                ],
                axis=1,
            )
            if own:
                keep[m * 256 : m * 256 + 168, :] = left
                keep[m * 256 + 168 : m * 256 + 256, :] = right
            else:
                send[m * 256 : m * 256 + 168, :] = left.astype(BF)
                send[m * 256 + 168 : m * 256 + 256, :] = right.astype(BF)


def scatter_shift(first, second, axis):
    step = {2: 16, 0: 4, 1: 1}[axis]
    at = row_ids() // step % 4
    down = pltpu.roll(second, step, 0)
    out = pltpu.roll(second, 64 - 3 * step, 0)
    return first + jnp.where(at == 0, 0.0, down), jnp.where(at == 0, out, 0.0)


def forward_kernel(
    lrules_in, lcodes_in, rrules_in, rcodes_in, split, weight,
    local, to_x, to_y, regions, sums, pack, lrules, lcodes, rrules, rcodes, sems,
):
    copies = fetch(
        (lrules_in, lcodes_in, rrules_in, rcodes_in), (lrules, lcodes, rrules, rcodes), sems
    )
    for shift in range(8):
        acc = None
        for index, tap in enumerate(TAPS):
            if tap_shift(tap) == shift:
                part = lax.dot_general(
                    split[tap_parity(tap)],
                    weight[:, index * 192 : (index + 1) * 192],
                    (((1,), (1,)), ((), ())),
                    preferred_element_type=F32,
                )
                acc = part if acc is None else acc + part
        for slot in range(3):
            regions[slot * 8 + shift] = acc[slot * 64 : slot * 64 + 64]
    for slot in range(3):
        for bit, axis in ((1, 0), (2, 1), (4, 2)):
            for other in range(8):
                if other & bit:
                    continue
                inner, outer = scatter_shift(
                    regions[slot * 8 + other], regions[slot * 8 + other + bit], axis
                )
                regions[slot * 8 + other] = inner
                regions[slot * 8 + other + bit] = outer
    for entry in range(16):
        sums[entry] = jnp.zeros((64, 192), F32)
    for copy in copies:
        copy.wait()
    for e in range(12):
        at = jnp.minimum(lrules[0, 0, 0, e], 2) * 8 + lcodes[0, 0, e]
        sums[lrules[0, 0, 1, e]] += regions[at]
    for m in range(3):
        for e in range(3):
            at = jnp.minimum(rrules[0, 0, m, 0, e], 2) * 8 + rcodes[0, m, 0, e]
            sums[(m + 1) * 4 + rrules[0, 0, m, 1, e]] += regions[at]
    for t in range(3):
        local[t] = sums[t]
        pack[16:32, :] = jnp.zeros((16, 192), F32)
        for r in range(4):
            pack[r * 4 : r * 4 + 4, :] = sums[4 + t, r * 16 : r * 16 + 4, :]
            pack[16 + r : 17 + r, :] = sums[12 + t, r * 16 : r * 16 + 1, :]
            for p in range(4):
                to_y[t, r * 4 + p : r * 4 + p + 1, :] = sums[
                    8 + t, r * 16 + p * 4 : r * 16 + p * 4 + 1, :
                ]
        to_x[t] = pack[...].astype(BF)


def join_kernel(to_y, got_x, out, rows):
    for t in range(3):
        edge = got_x[t].astype(F32)
        rows[...] = to_y[t]
        for r in range(4):
            rows[r * 4 : r * 4 + 1, :] += edge[16 + r : 17 + r]
        out[t] = rows[...].astype(BF)


def output_kernel(valid_in, local, got_x, got_y, out, acc, low, high, valid, sems):
    for copy in fetch((valid_in,), (valid,), sems):
        copy.wait()
    for t in range(3):
        acc[...] = local[t]
        from_x = got_x[t].astype(F32)
        from_y = got_y[t].astype(F32)
        for r in range(4):
            acc[r * 16 : r * 16 + 4, :] += from_x[r * 4 : r * 4 + 4]
        for row in range(16):
            acc[row * 4 : row * 4 + 1, :] += from_y[row : row + 1]
        live = valid[0, 0, t].astype(F32)
        for r in range(4):
            rows = acc[r * 16 : r * 16 + 16, :] * live
            put = pl.ds(r, 16, stride=4)
            low[put, :] = rows[:, 0:128]
            high[put, :] = jnp.concatenate([rows[:, 128:192], rows[:, 128:192]], axis=1)
        out[0, 0, t, :, 0:128] = low[...].astype(BF)
        out[0, 0, t, :, 128:192] = high[:, 0:64].astype(BF)


def features_kernel(valid_in, shifts, weight, out, cubes, valid, sems):
    for copy in fetch((valid_in,), (valid,), sems):
        copy.wait()
    for par in range(8):
        acc = None
        for index, tap in enumerate(TAPS):
            if tap_parity(tap) == par:
                part = jnp.dot(
                    shifts[tap_shift(tap)],
                    weight[:, index * 192 : (index + 1) * 192],
                    preferred_element_type=F32,
                )
                acc = part if acc is None else acc + part
        for slot in range(3):
            live = valid[0, 0, slot].astype(F32)
            rows = acc[slot * 64 : slot * 64 + 64] * live
            cubes[slot, par * 64 : par * 64 + 64, :] = rows.astype(BF)
    order = parity_order()
    for slot in range(3):
        out[0, 0, slot] = lax.dot_general(
            cubes[slot], order, (((0,), (0,)), ((), ())), preferred_element_type=F32
        ).astype(BF)


def share_kernel(mine, other, out, rows):
    full = mine[...].astype(F32) + other[...].astype(F32)
    rows[:, 0:128] = full[0:168]
    rows[0:88, 128:192] = full[168:256, 0:64]
    rows[88:168, 128:192] = full[176:256, 64:128]
    offset = lax.axis_index("gx") % 4 * 2
    for case in range(4):
        @pl.when(offset == case * 2)
        def _(case=case):
            out[...] = rows[case * 2 : case * 2 + 162, :]


def swap(value, axis, size, bits):
    return lax.ppermute(value, axis, [(i, i ^ bits) for i in range(size)])


def step(value, axis, sign):
    size = lax.axis_size(axis)
    route = [(i, i + sign) for i in range(size) if 0 <= i + sign < size]
    return lax.ppermute(value, axis, route)


def split_sum_kernel(count, mine, *refs):
    got, first, rest = refs[:count], refs[count], refs[count + 1 :]
    size = first.shape[0]
    for d in range(4):
        rows = slice(d * size, d * size + size)
        full = mine[rows, :]
        for ref in got:
            full = full + ref[rows, :].astype(F32)
        if d == 0:
            first[...] = full
        else:
            rest[d - 1][...] = full.astype(BF)


def split_sum(mine, got, limit):
    size = mine.shape[0] // 4
    outs = (jax.ShapeDtypeStruct((size, 128), F32),) + (jax.ShapeDtypeStruct((size, 128), BF),) * 3
    args = (mine, *got)
    kernel = functools.partial(split_sum_kernel, len(got))
    first, *rest = call(kernel, outs, args, (VM,) * len(args), [], 0, limit)
    return first, rest


def sum_kernel(first, one, two, three, out):
    total = first[...].astype(F32) + one[...].astype(F32)
    out[...] = (total + (two[...].astype(F32) + three[...].astype(F32))).astype(BF)


def sum_of(values):
    return call(sum_kernel, jax.ShapeDtypeStruct((256, 128), BF), values, (VM,) * 4, [], 0, 2)


def turns(parts, first_bits, second_bits):
    got = {}
    for d in (2, 3, 1):
        route = [(i, i ^ ((second_bits if i % 2 else first_bits) * d)) for i in range(32)]
        got[d] = lax.ppermute(parts[d - 1], "gx", route)
    return [got[1], got[2], got[3]]


def together(*values):
    return lax.optimization_barrier(values)


def shards(
    features, weight, cotangent, valid, local_rules, local_codes, remote_rules, remote_codes
):
    rules = (
        local_rules,
        local_codes,
        jnp.transpose(remote_rules, (0, 1, 3, 2, 4)),
        jnp.transpose(remote_codes, (0, 2, 1, 3)),
    )
    weight = weight.T
    features = jnp.swapaxes(features, 3, 4)
    shape = jax.ShapeDtypeStruct
    flops = 2 * 27 * 192**3
    masked, face = call(
        mask_kernel,
        (shape((3, 64, 192), BF), shape((3, 16, 192), BF)),
        (valid, cotangent),
        (HB, HB),
        [pltpu.VMEM((1, 1, 3, 64, 192), BF)] + scalars(FLAGS),
        0,
        2,
    )
    cot_x = step(face, "gx", -1)
    packed = call(pack_kernel, shape((3, 32, 192), BF), (masked, cot_x), (VM, VM), [], 0, 2)
    cot_y = step(packed, "gy", -1)
    split = call(
        split_kernel,
        shape((8, 192, 192), BF),
        (valid, together(features, packed)[0]),
        (HB, HB),
        [pltpu.VMEM((1, 1, 3, 192, 512), BF)] + scalars(FLAGS),
        0,
        6,
    )
    keep, send, shifts = call(
        weight_kernel,
        (shape((4096, 128), F32), shape((4096, 128), BF), shape((8, 192, 192), BF)),
        (*rules, split, masked, cot_x, cot_y),
        (HB,) * 4 + (VM,) * 4,
        [pltpu.VMEM((16, 64, 192), F32), pltpu.VMEM((32, 64, 192), F32)]
        + [pltpu.VMEM((64, 128), F32)] * 2
        + [pltpu.VMEM((5184, 192), F32)]
        + scalars(TABLES),
        flops,
        18,
    )
    send, split, weight = together(send, split, weight)
    arrived = swap(send, "gx", 32, 1)
    local, to_x, to_y = call(
        forward_kernel,
        (shape((3, 64, 192), F32), shape((3, 32, 192), BF), shape((3, 16, 192), F32)),
        (*rules, split, weight),
        (HB,) * 4 + (VM,) * 2,
        [pltpu.VMEM((24, 64, 192), F32), pltpu.VMEM((16, 64, 192), F32), pltpu.VMEM((32, 192), F32)]
        + scalars(TABLES),
        flops,
        12,
    )
    arrived, local, to_x, to_y = together(arrived, local, to_x, to_y)
    first, rest = split_sum(keep, [arrived], 8)
    rest, shifts, to_x = together(rest, shifts, to_x)
    arrived = turns(rest, 8, 2)
    got_x = step(to_x, "gx", 1)
    features_grad = call(
        features_kernel,
        shape((1, 1, 3, 192, 512), BF),
        (valid, shifts, weight),
        (HB, VM, VM),
        [pltpu.VMEM((3, 512, 192), BF)] + scalars(FLAGS),
        flops,
        12,
    )
    features_grad, got_x = together(features_grad, got_x)
    joined = call(
        join_kernel, shape((3, 16, 192), BF), (to_y, got_x), (VM, VM),
        [pltpu.VMEM((16, 192), F32)], 0, 2,
    )
    got_y = step(joined, "gy", 1)
    arrived, joined = together(arrived, joined)
    first, rest = split_sum(first, arrived, 4)
    part = sum_of((first, *turns(rest, 2, 8)))
    part = sum_of((part, *(swap(part, "gy", 8, d) for d in (1, 2, 3))))
    part, local = together(part, local)
    other = swap(part, "gy", 8, 4)
    output = call(
        output_kernel,
        shape((1, 1, 3, 64, 192), BF),
        (valid, local, got_x, got_y),
        (HB,) + (VM,) * 3,
        [pltpu.VMEM((64, 192), F32)] + [pltpu.VMEM((64, 128), F32)] * 2 + scalars(FLAGS),
        0,
    )
    other, output = together(other, output)
    weight_share = call(
        share_kernel,
        shape((162, 192), F32),
        (part, other),
        (VM, VM),
        [pltpu.VMEM((168, 192), F32)],
        0,
        2,
    )
    features_grad = jnp.swapaxes(features_grad, 3, 4)
    return output, features_grad, weight_share


def solution(mesh):
    return jax.shard_map(
        shards,
        mesh=mesh,
        in_specs=(
            P("gx", "gy", None, None, None),
            P(),
            P("gx", "gy", None, None, None),
            P("gx", "gy", None),
            P("gx", "gy", None, None),
            P("gx", "gy", None),
            P("gx", "gy", None, None, None),
            P("gx", "gy", None, None),
        ),
        out_specs=(P("gx", "gy", None, None, None), P("gx", "gy", None, None, None), P("gx", None)),
        check_vma=False,
    )
```

```python
import functools

import jax
import jax.numpy as jnp
from jax import lax
from jax.experimental import pallas as pl
from jax.experimental.pallas import tpu as pltpu
from jax.sharding import PartitionSpec as P


INTERPRET = False
BF = jnp.bfloat16
F32 = jnp.float32
VM = pltpu.MemorySpace.VMEM
HB = pltpu.MemorySpace.HBM
TABLES = ((1, 1, 2, 12), (1, 1, 12), (1, 1, 3, 2, 3), (1, 3, 1, 3))
FLAGS = ((1, 1, 3),)

PARITY = (1, 0, 1)
SHIFT = (1, 0, 0)
TAPS = [(e, f, g) for e in range(3) for f in range(3) for g in range(3)]


def tap_parity(tap):
    return PARITY[tap[0]] * 4 + PARITY[tap[1]] * 2 + PARITY[tap[2]]


def tap_shift(tap):
    return SHIFT[tap[0]] + 2 * SHIFT[tap[1]] + 4 * SHIFT[tap[2]]


def call(kernel, outs, args, spaces, scratch, flops, limit=4):
    nbytes = sum(a.size * a.dtype.itemsize for a in args)
    if not INTERPRET:
        args = [
            pltpu.with_memory_space_constraint(a, HB) if s == HB else a
            for a, s in zip(args, spaces)
        ]
    return pl.pallas_call(
        kernel,
        out_shape=outs,
        in_specs=[pl.BlockSpec(memory_space=s) for s in spaces],
        out_specs=jax.tree.map(lambda _: pl.BlockSpec(memory_space=VM), outs),
        scratch_shapes=scratch,
        compiler_params=pltpu.CompilerParams(vmem_limit_bytes=limit << 20),
        cost_estimate=pl.CostEstimate(flops=flops, bytes_accessed=nbytes, transcendentals=0),
        interpret=INTERPRET,
    )(*args)


def scalars(shapes):
    return [pltpu.SMEM(shape, jnp.int32) for shape in shapes] + [pltpu.SemaphoreType.DMA((8,))]


def fetch(sources, targets, sems):
    copies = [
        pltpu.make_async_copy(source, target, sems.at[n])
        for n, (source, target) in enumerate(zip(sources, targets))
    ]
    for copy in copies:
        copy.start()
    return copies


def parity_order():
    row = lax.broadcasted_iota(jnp.int32, (512, 512), 0)
    voxel = lax.broadcasted_iota(jnp.int32, (512, 512), 1)
    par, r, p, q = row >> 6, row >> 4 & 3, row >> 2 & 3, row & 3
    x = 2 * p + (par >> 2)
    y = 2 * q + (par >> 1 & 1)
    z = 2 * r + (par & 1)
    return jnp.where(voxel == x * 64 + y * 8 + z, 1.0, 0.0).astype(BF)


def split_kernel(valid_in, feat_in, out, feat, valid, sems):
    copies = fetch((valid_in, feat_in), (valid, feat), sems)
    order = parity_order()
    for copy in copies:
        copy.wait()
    for slot in range(3):
        rows = lax.dot_general(
            order, feat[0, 0, slot], (((1,), (1,)), ((), ())), preferred_element_type=F32
        )
        rows = (rows * valid[0, 0, slot].astype(F32)).astype(BF)
        for par in range(8):
            out[par, slot * 64 : slot * 64 + 64, :] = rows[par * 64 : par * 64 + 64]


def mask_kernel(valid_in, cot_in, masked, face_x, face_y, edge, cot, valid, sems):
    for copy in fetch((valid_in, cot_in), (valid, cot), sems):
        copy.wait()
    for slot in range(3):
        rows = cot[0, 0, slot].astype(F32) * valid[0, 0, slot].astype(F32)
        masked[slot] = rows.astype(BF)
        face_x[slot] = rows[0:16].astype(BF)
        face_y[slot] = jnp.concatenate(
            [rows[p * 16 : p * 16 + 4] for p in range(4)], axis=0
        ).astype(BF)
        edge[slot] = rows[0:8].astype(BF)


def row_ids():
    return lax.broadcasted_iota(jnp.int32, (64, 192), 0)


def gather_shift(first, second, axis):
    if axis == 2:
        return jnp.concatenate([first[16:], second[:16]], axis=0)
    step = 4 if axis == 0 else 1
    at = row_ids() // step % 4
    up = pltpu.roll(first, 64 - step, 0)
    wrap = pltpu.roll(second, 3 * step, 0)
    return jnp.where(at == 3, wrap, up)


def to_cube_order(cube, low, high):
    low[...] = cube[:, :128]
    high[:, 0:64] = cube[:, 128:]
    parts = []
    for r in range(4):
        take = pl.ds(r, 16, stride=4)
        parts.append(jnp.concatenate([low[take, :], high[take, :][:, 0:64]], axis=1))
    return jnp.concatenate(parts, axis=0)


def weight_kernel(
    lrules_in, lcodes_in, rrules_in, rcodes_in, split, masked, cot_x, cot_y, cot_xy,
    keep, send, shifts, cubes, grads, low, high, total, lrules, lcodes, rrules, rcodes, sems,
):
    copies = fetch(
        (lrules_in, lcodes_in, rrules_in, rcodes_in), (lrules, lcodes, rrules, rcodes), sems
    )
    zero = jnp.zeros((64, 192), F32)
    for group in range(16):
        cubes[group] = zero
    for slot in range(3):
        cubes[slot] = to_cube_order(masked[slot].astype(F32), low, high)
        from_x = cot_x[slot].astype(F32)
        from_y = cot_y[slot].astype(F32)
        from_xy = cot_xy[slot].astype(F32)
        for r in range(4):
            for n in range(4):
                put = slice(r * 16 + n, r * 16 + n + 1)
                cubes[4 + slot, put, :] = from_x[n * 4 + r : n * 4 + r + 1]
                put = slice(r * 16 + n * 4, r * 16 + n * 4 + 1)
                cubes[8 + slot, put, :] = from_y[n * 4 + r : n * 4 + r + 1]
            put = slice(r * 16, r * 16 + 1)
            cubes[12 + slot, put, :] = from_xy[r : r + 1]
    for entry in range(32):
        grads[entry] = zero
    for copy in copies:
        copy.wait()
    for e in range(12):
        at = lrules[0, 0, 0, e] * 8 + lcodes[0, 0, e]
        grads[at] += cubes[lrules[0, 0, 1, e]]
    for m in range(3):
        for e in range(3):
            at = rrules[0, 0, m, 0, e] * 8 + rcodes[0, m, 0, e]
            grads[at] += cubes[(m + 1) * 4 + rrules[0, 0, m, 1, e]]
    for slot in range(3):
        level = {}
        for u in range(2):
            for v in range(2):
                first = grads[slot * 8 + u + 2 * v]
                second = grads[slot * 8 + u + 2 * v + 4]
                level[u, v, 0] = first
                level[u, v, 1] = gather_shift(first, second, 2)
        after = {}
        for v in range(2):
            for w in range(2):
                after[0, v, w] = level[0, v, w]
                after[1, v, w] = gather_shift(level[0, v, w], level[1, v, w], 0)
        for u in range(2):
            for w in range(2):
                rows = slice(slot * 64, slot * 64 + 64)
                shifts[u + 4 * w, rows, :] = after[u, 0, w].astype(BF)
                shifts[u + 2 + 4 * w, rows, :] = gather_shift(
                    after[u, 0, w], after[u, 1, w], 1
                ).astype(BF)
    for index, tap in enumerate(TAPS):
        total[index * 192 : (index + 1) * 192, :] = lax.dot_general(
            split[tap_parity(tap)],
            shifts[tap_shift(tap)],
            (((0,), (0,)), ((), ())),
            preferred_element_type=F32,
        )
    here = lax.axis_index("gx")
    core = here % 2
    for m in range(16):
        other = m % 4 * 4 + m // 4
        for own in range(2):
            keeper = core if own else 1 - core
            block = ((here // 2) ^ jnp.where(keeper == 0, m, other)) * 2 + keeper
            start = pl.multiple_of(block * 162 // 8 * 8, 8)
            left = total[pl.ds(start, 168), 0:128]
            right = jnp.concatenate(
                [
                    total[pl.ds(start, 88), 128:192],
                    total[pl.ds(pl.multiple_of(start + 80, 8), 88), 128:192],
                ],
                axis=1,
            )
            if own:
                keep[m * 256 : m * 256 + 168, :] = left
                keep[m * 256 + 168 : m * 256 + 256, :] = right
            else:
                send[m * 256 : m * 256 + 168, :] = left.astype(BF)
                send[m * 256 + 168 : m * 256 + 256, :] = right.astype(BF)


def scatter_shift(first, second, axis):
    step = {2: 16, 0: 4, 1: 1}[axis]
    at = row_ids() // step % 4
    down = pltpu.roll(second, step, 0)
    out = pltpu.roll(second, 64 - 3 * step, 0)
    return first + jnp.where(at == 0, 0.0, down), jnp.where(at == 0, out, 0.0)


def forward_kernel(
    lrules_in, lcodes_in, rrules_in, rcodes_in, split, weight,
    local, to_x, to_y, regions, sums, pack, lrules, lcodes, rrules, rcodes, sems,
):
    copies = fetch(
        (lrules_in, lcodes_in, rrules_in, rcodes_in), (lrules, lcodes, rrules, rcodes), sems
    )
    for shift in range(8):
        acc = None
        for index, tap in enumerate(TAPS):
            if tap_shift(tap) == shift:
                part = lax.dot_general(
                    split[tap_parity(tap)],
                    weight[:, index * 192 : (index + 1) * 192],
                    (((1,), (1,)), ((), ())),
                    preferred_element_type=F32,
                )
                acc = part if acc is None else acc + part
        for slot in range(3):
            regions[slot * 8 + shift] = acc[slot * 64 : slot * 64 + 64]
    for slot in range(3):
        for bit, axis in ((1, 0), (2, 1), (4, 2)):
            for other in range(8):
                if other & bit:
                    continue
                inner, outer = scatter_shift(
                    regions[slot * 8 + other], regions[slot * 8 + other + bit], axis
                )
                regions[slot * 8 + other] = inner
                regions[slot * 8 + other + bit] = outer
    for entry in range(16):
        sums[entry] = jnp.zeros((64, 192), F32)
    for copy in copies:
        copy.wait()
    for e in range(12):
        at = jnp.minimum(lrules[0, 0, 0, e], 2) * 8 + lcodes[0, 0, e]
        sums[lrules[0, 0, 1, e]] += regions[at]
    for m in range(3):
        for e in range(3):
            at = jnp.minimum(rrules[0, 0, m, 0, e], 2) * 8 + rcodes[0, m, 0, e]
            sums[(m + 1) * 4 + rrules[0, 0, m, 1, e]] += regions[at]
    for t in range(3):
        local[t] = sums[t]
        pack[16:32, :] = jnp.zeros((16, 192), F32)
        for r in range(4):
            pack[r * 4 : r * 4 + 4, :] = sums[4 + t, r * 16 : r * 16 + 4, :]
            pack[16 + r : 17 + r, :] = sums[12 + t, r * 16 : r * 16 + 1, :]
            for p in range(4):
                to_y[t, r * 4 + p : r * 4 + p + 1, :] = sums[
                    8 + t, r * 16 + p * 4 : r * 16 + p * 4 + 1, :
                ]
        to_x[t] = pack[...].astype(BF)


def join_kernel(to_y, got_x, out, rows):
    for t in range(3):
        edge = got_x[t].astype(F32)
        rows[...] = to_y[t]
        for r in range(4):
            rows[r * 4 : r * 4 + 1, :] += edge[16 + r : 17 + r]
        out[t] = rows[...].astype(BF)


def output_kernel(valid_in, local, got_x, got_y, out, acc, low, high, valid, sems):
    for copy in fetch((valid_in,), (valid,), sems):
        copy.wait()
    for t in range(3):
        acc[...] = local[t]
        from_x = got_x[t].astype(F32)
        from_y = got_y[t].astype(F32)
        for r in range(4):
            acc[r * 16 : r * 16 + 4, :] += from_x[r * 4 : r * 4 + 4]
        for row in range(16):
            acc[row * 4 : row * 4 + 1, :] += from_y[row : row + 1]
        live = valid[0, 0, t].astype(F32)
        for r in range(4):
            rows = acc[r * 16 : r * 16 + 16, :] * live
            put = pl.ds(r, 16, stride=4)
            low[put, :] = rows[:, 0:128]
            high[put, :] = jnp.concatenate([rows[:, 128:192], rows[:, 128:192]], axis=1)
        out[0, 0, t, :, 0:128] = low[...].astype(BF)
        out[0, 0, t, :, 128:192] = high[:, 0:64].astype(BF)


def features_kernel(valid_in, shifts, weight, out, cubes, valid, sems):
    for copy in fetch((valid_in,), (valid,), sems):
        copy.wait()
    for par in range(8):
        acc = None
        for index, tap in enumerate(TAPS):
            if tap_parity(tap) == par:
                part = jnp.dot(
                    shifts[tap_shift(tap)],
                    weight[:, index * 192 : (index + 1) * 192],
                    preferred_element_type=F32,
                )
                acc = part if acc is None else acc + part
        for slot in range(3):
            live = valid[0, 0, slot].astype(F32)
            rows = acc[slot * 64 : slot * 64 + 64] * live
            cubes[slot, par * 64 : par * 64 + 64, :] = rows.astype(BF)
    order = parity_order()
    for slot in range(3):
        out[0, 0, slot] = lax.dot_general(
            cubes[slot], order, (((0,), (0,)), ((), ())), preferred_element_type=F32
        ).astype(BF)


def share_kernel(mine, other, out, rows):
    full = mine[...].astype(F32) + other[...].astype(F32)
    rows[:, 0:128] = full[0:168]
    rows[0:88, 128:192] = full[168:256, 0:64]
    rows[88:168, 128:192] = full[176:256, 64:128]
    offset = lax.axis_index("gx") % 4 * 2
    for case in range(4):
        @pl.when(offset == case * 2)
        def _(case=case):
            out[...] = rows[case * 2 : case * 2 + 162, :]


def swap(value, axis, size, bits):
    return lax.ppermute(value, axis, [(i, i ^ bits) for i in range(size)])


def step(value, axis, sign):
    size = lax.axis_size(axis)
    route = [(i, i + sign) for i in range(size) if 0 <= i + sign < size]
    return lax.ppermute(value, axis, route)


def split_sum_kernel(count, mine, *refs):
    got, first, rest = refs[:count], refs[count], refs[count + 1 :]
    size = first.shape[0]
    for d in range(4):
        rows = slice(d * size, d * size + size)
        full = mine[rows, :]
        for ref in got:
            full = full + ref[rows, :].astype(F32)
        if d == 0:
            first[...] = full
        else:
            rest[d - 1][...] = full.astype(BF)


def split_sum(mine, got, limit):
    size = mine.shape[0] // 4
    outs = (jax.ShapeDtypeStruct((size, 128), F32),) + (jax.ShapeDtypeStruct((size, 128), BF),) * 3
    args = (mine, *got)
    kernel = functools.partial(split_sum_kernel, len(got))
    first, *rest = call(kernel, outs, args, (VM,) * len(args), [], 0, limit)
    return first, rest


def sum_kernel(first, one, two, three, out):
    total = first[...].astype(F32) + one[...].astype(F32)
    out[...] = (total + (two[...].astype(F32) + three[...].astype(F32))).astype(BF)


def sum_of(values):
    return call(sum_kernel, jax.ShapeDtypeStruct((256, 128), BF), values, (VM,) * 4, [], 0, 2)


def turns(parts, first_bits, second_bits):
    got = {}
    for d in (2, 3, 1):
        route = [(i, i ^ ((second_bits if i % 2 else first_bits) * d)) for i in range(32)]
        got[d] = lax.ppermute(parts[d - 1], "gx", route)
    return [got[1], got[2], got[3]]


def together(*values):
    return lax.optimization_barrier(values)


def shards(
    features, weight, cotangent, valid, local_rules, local_codes, remote_rules, remote_codes
):
    rules = (
        local_rules,
        local_codes,
        jnp.transpose(remote_rules, (0, 1, 3, 2, 4)),
        jnp.transpose(remote_codes, (0, 2, 1, 3)),
    )
    weight = weight.T
    features = jnp.swapaxes(features, 3, 4)
    shape = jax.ShapeDtypeStruct
    flops = 2 * 27 * 192**3
    masked, face_x, face_y, edge = call(
        mask_kernel,
        (shape((3, 64, 192), BF),) + (shape((3, 16, 192), BF),) * 2 + (shape((3, 8, 192), BF),),
        (valid, cotangent),
        (HB, HB),
        [pltpu.VMEM((1, 1, 3, 64, 192), BF)] + scalars(FLAGS),
        0,
        2,
    )
    cot_y = step(face_y, "gy", -1)
    columns = lax.axis_size("gy")
    route = [
        (i * columns + j, (i - 1) * columns + j - 1)
        for i in range(1, lax.axis_size("gx"))
        for j in range(1, columns)
    ]
    cot_xy = lax.ppermute(edge, ("gx", "gy"), route)
    cot_x = step(face_x, "gx", -1)
    split = call(
        split_kernel,
        shape((8, 192, 192), BF),
        (valid, together(features, edge)[0]),
        (HB, HB),
        [pltpu.VMEM((1, 1, 3, 192, 512), BF)] + scalars(FLAGS),
        0,
        6,
    )
    keep, send, shifts = call(
        weight_kernel,
        (shape((4096, 128), F32), shape((4096, 128), BF), shape((8, 192, 192), BF)),
        (*rules, split, masked, cot_x, cot_y, cot_xy),
        (HB,) * 4 + (VM,) * 5,
        [pltpu.VMEM((16, 64, 192), F32), pltpu.VMEM((32, 64, 192), F32)]
        + [pltpu.VMEM((64, 128), F32)] * 2
        + [pltpu.VMEM((5184, 192), F32)]
        + scalars(TABLES),
        flops,
        18,
    )
    send, split, weight = together(send, split, weight)
    arrived = swap(send, "gx", 32, 1)
    local, to_x, to_y = call(
        forward_kernel,
        (shape((3, 64, 192), F32), shape((3, 32, 192), BF), shape((3, 16, 192), F32)),
        (*rules, split, weight),
        (HB,) * 4 + (VM,) * 2,
        [pltpu.VMEM((24, 64, 192), F32), pltpu.VMEM((16, 64, 192), F32), pltpu.VMEM((32, 192), F32)]
        + scalars(TABLES),
        flops,
        12,
    )
    arrived, local, to_x, to_y = together(arrived, local, to_x, to_y)
    first, rest = split_sum(keep, [arrived], 8)
    rest, shifts, to_x = together(rest, shifts, to_x)
    arrived = turns(rest, 8, 2)
    got_x = step(to_x, "gx", 1)
    features_grad = call(
        features_kernel,
        shape((1, 1, 3, 192, 512), BF),
        (valid, shifts, weight),
        (HB, VM, VM),
        [pltpu.VMEM((3, 512, 192), BF)] + scalars(FLAGS),
        flops,
        12,
    )
    arrived, features_grad = together(arrived, features_grad)
    first, rest = split_sum(first, arrived, 4)
    part = sum_of((first, *turns(rest, 2, 8)))
    part, to_y = together(part, to_y)
    got = [swap(part, "gy", 8, d) for d in (1, 2, 3)]
    joined = call(
        join_kernel, shape((3, 16, 192), BF), (to_y, got_x), (VM, VM),
        [pltpu.VMEM((16, 192), F32)], 0, 2,
    )
    got_y = step(joined, "gy", 1)
    part = sum_of((part, *got))
    part, local = together(part, local)
    other = swap(part, "gy", 8, 4)
    output = call(
        output_kernel,
        shape((1, 1, 3, 64, 192), BF),
        (valid, local, got_x, got_y),
        (HB,) + (VM,) * 3,
        [pltpu.VMEM((64, 192), F32)] + [pltpu.VMEM((64, 128), F32)] * 2 + scalars(FLAGS),
        0,
    )
    other, output = together(other, output)
    weight_share = call(
        share_kernel,
        shape((162, 192), F32),
        (part, other),
        (VM, VM),
        [pltpu.VMEM((168, 192), F32)],
        0,
        2,
    )
    features_grad = jnp.swapaxes(features_grad, 3, 4)
    return output, features_grad, weight_share


def solution(mesh):
    return jax.shard_map(
        shards,
        mesh=mesh,
        in_specs=(
            P("gx", "gy", None, None, None),
            P(),
            P("gx", "gy", None, None, None),
            P("gx", "gy", None),
            P("gx", "gy", None, None),
            P("gx", "gy", None),
            P("gx", "gy", None, None, None),
            P("gx", "gy", None, None),
        ),
        out_specs=(P("gx", "gy", None, None, None), P("gx", "gy", None, None, None), P("gx", None)),
        check_vma=False,
    )
```

```python
import functools

import jax
import jax.numpy as jnp
from jax import lax
from jax.experimental import pallas as pl
from jax.experimental.pallas import tpu as pltpu
from jax.sharding import PartitionSpec as P


INTERPRET = False
BF = jnp.bfloat16
F32 = jnp.float32
VM = pltpu.MemorySpace.VMEM
HB = pltpu.MemorySpace.HBM
TABLES = ((1, 1, 2, 12), (1, 1, 12), (1, 1, 3, 2, 3), (1, 3, 1, 3))
FLAGS = ((1, 1, 3),)

PARITY = (1, 0, 1)
SHIFT = (1, 0, 0)
TAPS = [(e, f, g) for e in range(3) for f in range(3) for g in range(3)]


def tap_parity(tap):
    return PARITY[tap[0]] * 4 + PARITY[tap[1]] * 2 + PARITY[tap[2]]


def tap_shift(tap):
    return SHIFT[tap[0]] + 2 * SHIFT[tap[1]] + 4 * SHIFT[tap[2]]


def call(kernel, outs, args, spaces, scratch, flops, limit=4):
    nbytes = sum(a.size * a.dtype.itemsize for a in args)
    if not INTERPRET:
        args = [
            pltpu.with_memory_space_constraint(a, HB) if s == HB else a
            for a, s in zip(args, spaces)
        ]
    return pl.pallas_call(
        kernel,
        out_shape=outs,
        in_specs=[pl.BlockSpec(memory_space=s) for s in spaces],
        out_specs=jax.tree.map(lambda _: pl.BlockSpec(memory_space=VM), outs),
        scratch_shapes=scratch,
        compiler_params=pltpu.CompilerParams(vmem_limit_bytes=limit << 20),
        cost_estimate=pl.CostEstimate(flops=flops, bytes_accessed=nbytes, transcendentals=0),
        interpret=INTERPRET,
    )(*args)


def scalars(shapes):
    return [pltpu.SMEM(shape, jnp.int32) for shape in shapes] + [pltpu.SemaphoreType.DMA((8,))]


def fetch(sources, targets, sems):
    copies = [
        pltpu.make_async_copy(source, target, sems.at[n])
        for n, (source, target) in enumerate(zip(sources, targets))
    ]
    for copy in copies:
        copy.start()
    return copies


def parity_order():
    row = lax.broadcasted_iota(jnp.int32, (512, 512), 0)
    voxel = lax.broadcasted_iota(jnp.int32, (512, 512), 1)
    par, r, p, q = row >> 6, row >> 4 & 3, row >> 2 & 3, row & 3
    x = 2 * p + (par >> 2)
    y = 2 * q + (par >> 1 & 1)
    z = 2 * r + (par & 1)
    return jnp.where(voxel == x * 64 + y * 8 + z, 1.0, 0.0).astype(BF)


def split_kernel(valid_in, feat_in, weight_in, out, weight, feat, valid, sems):
    copies = fetch((valid_in, feat_in, weight_in), (valid, feat, weight), sems)
    order = parity_order()
    for copy in copies[:2]:
        copy.wait()
    for slot in range(3):
        rows = lax.dot_general(
            order, feat[0, 0, slot], (((1,), (1,)), ((), ())), preferred_element_type=F32
        )
        rows = (rows * valid[0, 0, slot].astype(F32)).astype(BF)
        for par in range(8):
            out[par, slot * 64 : slot * 64 + 64, :] = rows[par * 64 : par * 64 + 64]
    copies[2].wait()


def mask_kernel(valid_in, cot_in, masked, face_x, face_y, edge, cot, valid, sems):
    for copy in fetch((valid_in, cot_in), (valid, cot), sems):
        copy.wait()
    for slot in range(3):
        rows = cot[0, 0, slot].astype(F32) * valid[0, 0, slot].astype(F32)
        masked[slot] = rows.astype(BF)
        face_x[slot] = rows[0:16].astype(BF)
        face_y[slot] = jnp.concatenate(
            [rows[p * 16 : p * 16 + 4] for p in range(4)], axis=0
        ).astype(BF)
        edge[slot] = rows[0:8].astype(BF)


def row_ids():
    return lax.broadcasted_iota(jnp.int32, (64, 192), 0)


def gather_shift(first, second, axis):
    if axis == 2:
        return jnp.concatenate([first[16:], second[:16]], axis=0)
    step = 4 if axis == 0 else 1
    at = row_ids() // step % 4
    up = pltpu.roll(first, 64 - step, 0)
    wrap = pltpu.roll(second, 3 * step, 0)
    return jnp.where(at == 3, wrap, up)


def to_cube_order(cube, low, high):
    low[...] = cube[:, :128]
    high[:, 0:64] = cube[:, 128:]
    parts = []
    for r in range(4):
        take = pl.ds(r, 16, stride=4)
        parts.append(jnp.concatenate([low[take, :], high[take, :][:, 0:64]], axis=1))
    return jnp.concatenate(parts, axis=0)


def weight_kernel(
    lrules_in, lcodes_in, rrules_in, rcodes_in, split, masked, cot_x, cot_y, cot_xy,
    keep, send, shifts, cubes, grads, low, high, total, lrules, lcodes, rrules, rcodes, sems,
):
    copies = fetch(
        (lrules_in, lcodes_in, rrules_in, rcodes_in), (lrules, lcodes, rrules, rcodes), sems
    )
    zero = jnp.zeros((64, 192), F32)
    for group in range(16):
        cubes[group] = zero
    for slot in range(3):
        cubes[slot] = to_cube_order(masked[slot].astype(F32), low, high)
        from_x = cot_x[slot].astype(F32)
        from_y = cot_y[slot].astype(F32)
        from_xy = cot_xy[slot].astype(F32)
        for r in range(4):
            for n in range(4):
                put = slice(r * 16 + n, r * 16 + n + 1)
                cubes[4 + slot, put, :] = from_x[n * 4 + r : n * 4 + r + 1]
                put = slice(r * 16 + n * 4, r * 16 + n * 4 + 1)
                cubes[8 + slot, put, :] = from_y[n * 4 + r : n * 4 + r + 1]
            put = slice(r * 16, r * 16 + 1)
            cubes[12 + slot, put, :] = from_xy[r : r + 1]
    for entry in range(32):
        grads[entry] = zero
    for copy in copies:
        copy.wait()
    for e in range(12):
        at = lrules[0, 0, 0, e] * 8 + lcodes[0, 0, e]
        grads[at] += cubes[lrules[0, 0, 1, e]]
    for m in range(3):
        for e in range(3):
            at = rrules[0, 0, m, 0, e] * 8 + rcodes[0, m, 0, e]
            grads[at] += cubes[(m + 1) * 4 + rrules[0, 0, m, 1, e]]
    for slot in range(3):
        level = {}
        for u in range(2):
            for v in range(2):
                first = grads[slot * 8 + u + 2 * v]
                second = grads[slot * 8 + u + 2 * v + 4]
                level[u, v, 0] = first
                level[u, v, 1] = gather_shift(first, second, 2)
        after = {}
        for v in range(2):
            for w in range(2):
                after[0, v, w] = level[0, v, w]
                after[1, v, w] = gather_shift(level[0, v, w], level[1, v, w], 0)
        for u in range(2):
            for w in range(2):
                rows = slice(slot * 64, slot * 64 + 64)
                shifts[u + 4 * w, rows, :] = after[u, 0, w].astype(BF)
                shifts[u + 2 + 4 * w, rows, :] = gather_shift(
                    after[u, 0, w], after[u, 1, w], 1
                ).astype(BF)
    for index, tap in enumerate(TAPS):
        total[index * 192 : (index + 1) * 192, :] = lax.dot_general(
            split[tap_parity(tap)],
            shifts[tap_shift(tap)],
            (((0,), (0,)), ((), ())),
            preferred_element_type=F32,
        )
    here = lax.axis_index("gx")
    core = here % 2
    for m in range(16):
        other = m % 4 * 4 + m // 4
        for own in range(2):
            keeper = core if own else 1 - core
            block = ((here // 2) ^ jnp.where(keeper == 0, m, other)) * 2 + keeper
            start = pl.multiple_of(block * 162 // 8 * 8, 8)
            left = total[pl.ds(start, 168), 0:128]
            right = jnp.concatenate(
                [
                    total[pl.ds(start, 88), 128:192],
                    total[pl.ds(pl.multiple_of(start + 80, 8), 88), 128:192],
                ],
                axis=1,
            )
            if own:
                keep[m * 256 : m * 256 + 168, :] = left
                keep[m * 256 + 168 : m * 256 + 256, :] = right
            else:
                send[m * 256 : m * 256 + 168, :] = left.astype(BF)
                send[m * 256 + 168 : m * 256 + 256, :] = right.astype(BF)


def scatter_shift(first, second, axis):
    step = {2: 16, 0: 4, 1: 1}[axis]
    at = row_ids() // step % 4
    down = pltpu.roll(second, step, 0)
    out = pltpu.roll(second, 64 - 3 * step, 0)
    return first + jnp.where(at == 0, 0.0, down), jnp.where(at == 0, out, 0.0)


def forward_kernel(
    lrules_in, lcodes_in, rrules_in, rcodes_in, split, weight,
    local, to_x, to_y, regions, sums, pack, lrules, lcodes, rrules, rcodes, sems,
):
    copies = fetch(
        (lrules_in, lcodes_in, rrules_in, rcodes_in), (lrules, lcodes, rrules, rcodes), sems
    )
    for shift in range(8):
        acc = None
        for index, tap in enumerate(TAPS):
            if tap_shift(tap) == shift:
                part = lax.dot_general(
                    split[tap_parity(tap)],
                    weight[:, index * 192 : (index + 1) * 192],
                    (((1,), (1,)), ((), ())),
                    preferred_element_type=F32,
                )
                acc = part if acc is None else acc + part
        for slot in range(3):
            regions[slot * 8 + shift] = acc[slot * 64 : slot * 64 + 64]
    for slot in range(3):
        for bit, axis in ((1, 0), (2, 1), (4, 2)):
            for other in range(8):
                if other & bit:
                    continue
                inner, outer = scatter_shift(
                    regions[slot * 8 + other], regions[slot * 8 + other + bit], axis
                )
                regions[slot * 8 + other] = inner
                regions[slot * 8 + other + bit] = outer
    for entry in range(16):
        sums[entry] = jnp.zeros((64, 192), F32)
    for copy in copies:
        copy.wait()
    for e in range(12):
        at = jnp.minimum(lrules[0, 0, 0, e], 2) * 8 + lcodes[0, 0, e]
        sums[lrules[0, 0, 1, e]] += regions[at]
    for m in range(3):
        for e in range(3):
            at = jnp.minimum(rrules[0, 0, m, 0, e], 2) * 8 + rcodes[0, m, 0, e]
            sums[(m + 1) * 4 + rrules[0, 0, m, 1, e]] += regions[at]
    for t in range(3):
        local[t] = sums[t]
        pack[16:32, :] = jnp.zeros((16, 192), F32)
        for r in range(4):
            pack[r * 4 : r * 4 + 4, :] = sums[4 + t, r * 16 : r * 16 + 4, :]
            pack[16 + r : 17 + r, :] = sums[12 + t, r * 16 : r * 16 + 1, :]
            for p in range(4):
                to_y[t, r * 4 + p : r * 4 + p + 1, :] = sums[
                    8 + t, r * 16 + p * 4 : r * 16 + p * 4 + 1, :
                ]
        to_x[t] = pack[...].astype(BF)


def join_kernel(to_y, got_x, out, rows):
    for t in range(3):
        edge = got_x[t].astype(F32)
        rows[...] = to_y[t]
        for r in range(4):
            rows[r * 4 : r * 4 + 1, :] += edge[16 + r : 17 + r]
        out[t] = rows[...].astype(BF)


def output_kernel(valid_in, local, got_x, got_y, out, acc, low, high, valid, sems):
    for copy in fetch((valid_in,), (valid,), sems):
        copy.wait()
    for t in range(3):
        acc[...] = local[t]
        from_x = got_x[t].astype(F32)
        from_y = got_y[t].astype(F32)
        for r in range(4):
            acc[r * 16 : r * 16 + 4, :] += from_x[r * 4 : r * 4 + 4]
        for row in range(16):
            acc[row * 4 : row * 4 + 1, :] += from_y[row : row + 1]
        live = valid[0, 0, t].astype(F32)
        for r in range(4):
            rows = acc[r * 16 : r * 16 + 16, :] * live
            put = pl.ds(r, 16, stride=4)
            low[put, :] = rows[:, 0:128]
            high[put, :] = jnp.concatenate([rows[:, 128:192], rows[:, 128:192]], axis=1)
        out[0, 0, t, :, 0:128] = low[...].astype(BF)
        out[0, 0, t, :, 128:192] = high[:, 0:64].astype(BF)


def features_kernel(valid_in, shifts, weight, out, cubes, valid, sems):
    for copy in fetch((valid_in,), (valid,), sems):
        copy.wait()
    for par in range(8):
        acc = None
        for index, tap in enumerate(TAPS):
            if tap_parity(tap) == par:
                part = jnp.dot(
                    shifts[tap_shift(tap)],
                    weight[:, index * 192 : (index + 1) * 192],
                    preferred_element_type=F32,
                )
                acc = part if acc is None else acc + part
        for slot in range(3):
            live = valid[0, 0, slot].astype(F32)
            rows = acc[slot * 64 : slot * 64 + 64] * live
            cubes[slot, par * 64 : par * 64 + 64, :] = rows.astype(BF)
    order = parity_order()
    for slot in range(3):
        out[0, 0, slot] = lax.dot_general(
            cubes[slot], order, (((0,), (0,)), ((), ())), preferred_element_type=F32
        ).astype(BF)


def share_kernel(mine, other, out, rows):
    full = mine[...].astype(F32) + other[...].astype(F32)
    rows[:, 0:128] = full[0:168]
    rows[0:88, 128:192] = full[168:256, 0:64]
    rows[88:168, 128:192] = full[176:256, 64:128]
    offset = lax.axis_index("gx") % 4 * 2
    for case in range(4):
        @pl.when(offset == case * 2)
        def _(case=case):
            out[...] = rows[case * 2 : case * 2 + 162, :]


def swap(value, axis, size, bits):
    return lax.ppermute(value, axis, [(i, i ^ bits) for i in range(size)])


def step(value, axis, sign):
    size = lax.axis_size(axis)
    route = [(i, i + sign) for i in range(size) if 0 <= i + sign < size]
    return lax.ppermute(value, axis, route)


def split_sum_kernel(count, mine, *refs):
    got, first, rest = refs[:count], refs[count], refs[count + 1 :]
    size = first.shape[0]
    for d in range(4):
        rows = slice(d * size, d * size + size)
        full = mine[rows, :]
        for ref in got:
            full = full + ref[rows, :].astype(F32)
        if d == 0:
            first[...] = full
        else:
            rest[d - 1][...] = full.astype(BF)


def split_sum(mine, got, limit):
    size = mine.shape[0] // 4
    outs = (jax.ShapeDtypeStruct((size, 128), F32),) + (jax.ShapeDtypeStruct((size, 128), BF),) * 3
    args = (mine, *got)
    kernel = functools.partial(split_sum_kernel, len(got))
    first, *rest = call(kernel, outs, args, (VM,) * len(args), [], 0, limit)
    return first, rest


def sum_kernel(first, one, two, three, out):
    total = first[...].astype(F32) + one[...].astype(F32)
    out[...] = (total + (two[...].astype(F32) + three[...].astype(F32))).astype(BF)


def sum_of(values):
    return call(sum_kernel, jax.ShapeDtypeStruct((256, 128), BF), values, (VM,) * 4, [], 0, 2)


def turns(parts, first_bits, second_bits):
    got = {}
    for d in (2, 3, 1):
        route = [(i, i ^ ((second_bits if i % 2 else first_bits) * d)) for i in range(32)]
        got[d] = lax.ppermute(parts[d - 1], "gx", route)
    return [got[1], got[2], got[3]]


def together(*values):
    return lax.optimization_barrier(values)


def shards(
    features, weight, cotangent, valid, local_rules, local_codes, remote_rules, remote_codes
):
    rules = (
        local_rules,
        local_codes,
        jnp.transpose(remote_rules, (0, 1, 3, 2, 4)),
        jnp.transpose(remote_codes, (0, 2, 1, 3)),
    )
    weight = weight.T
    features = jnp.swapaxes(features, 3, 4)
    shape = jax.ShapeDtypeStruct
    flops = 2 * 27 * 192**3
    masked, face_x, face_y, edge = call(
        mask_kernel,
        (shape((3, 64, 192), BF),) + (shape((3, 16, 192), BF),) * 2 + (shape((3, 8, 192), BF),),
        (valid, cotangent),
        (HB, HB),
        [pltpu.VMEM((1, 1, 3, 64, 192), BF)] + scalars(FLAGS),
        0,
        2,
    )
    cot_y = step(face_y, "gy", -1)
    columns = lax.axis_size("gy")
    route = [
        (i * columns + j, (i - 1) * columns + j - 1)
        for i in range(1, lax.axis_size("gx"))
        for j in range(1, columns)
    ]
    cot_xy = lax.ppermute(edge, ("gx", "gy"), route)
    cot_x = step(face_x, "gx", -1)
    split, weight = call(
        split_kernel,
        (shape((8, 192, 192), BF), shape((192, 5184), BF)),
        (valid, together(features, edge)[0], weight),
        (HB,) * 3,
        [pltpu.VMEM((1, 1, 3, 192, 512), BF)] + scalars(FLAGS),
        flops,
        10,
    )
    local, to_x, to_y = call(
        forward_kernel,
        (shape((3, 64, 192), F32), shape((3, 32, 192), BF), shape((3, 16, 192), F32)),
        (*rules, split, weight),
        (HB,) * 4 + (VM,) * 2,
        [pltpu.VMEM((24, 64, 192), F32), pltpu.VMEM((16, 64, 192), F32), pltpu.VMEM((32, 192), F32)]
        + scalars(TABLES),
        flops,
        12,
    )
    split, local, to_x, to_y = together(split, local, to_x, to_y)
    keep, send, shifts = call(
        weight_kernel,
        (shape((4096, 128), F32), shape((4096, 128), BF), shape((8, 192, 192), BF)),
        (*rules, split, masked, cot_x, cot_y, cot_xy),
        (HB,) * 4 + (VM,) * 5,
        [pltpu.VMEM((16, 64, 192), F32), pltpu.VMEM((32, 64, 192), F32)]
        + [pltpu.VMEM((64, 128), F32)] * 2
        + [pltpu.VMEM((5184, 192), F32)]
        + scalars(TABLES),
        flops,
        18,
    )
    send, to_x = together(send, to_x)
    arrived = swap(send, "gx", 32, 1)
    got_x = step(to_x, "gx", 1)
    first, rest = split_sum(keep, [arrived], 8)
    rest, shifts = together(rest, shifts)
    arrived = turns(rest, 8, 2)
    features_grad = call(
        features_kernel,
        shape((1, 1, 3, 192, 512), BF),
        (valid, shifts, weight),
        (HB, VM, VM),
        [pltpu.VMEM((3, 512, 192), BF)] + scalars(FLAGS),
        flops,
        12,
    )
    features_grad, got_x, to_y = together(features_grad, got_x, to_y)
    joined = call(
        join_kernel, shape((3, 16, 192), BF), (to_y, got_x), (VM, VM),
        [pltpu.VMEM((16, 192), F32)], 0, 2,
    )
    got_y = step(joined, "gy", 1)
    arrived, features_grad = together(arrived, features_grad)
    first, rest = split_sum(first, arrived, 4)
    part = sum_of((first, *turns(rest, 2, 8)))
    got = [swap(part, "gy", 8, d) for d in (1, 2, 3)]
    part = sum_of((part, *got))
    part, local = together(part, local)
    other = swap(part, "gy", 8, 4)
    output = call(
        output_kernel,
        shape((1, 1, 3, 64, 192), BF),
        (valid, local, got_x, got_y),
        (HB,) + (VM,) * 3,
        [pltpu.VMEM((64, 192), F32)] + [pltpu.VMEM((64, 128), F32)] * 2 + scalars(FLAGS),
        0,
    )
    other, output = together(other, output)
    weight_share = call(
        share_kernel,
        shape((162, 192), F32),
        (part, other),
        (VM, VM),
        [pltpu.VMEM((168, 192), F32)],
        0,
        2,
    )
    features_grad = jnp.swapaxes(features_grad, 3, 4)
    return output, features_grad, weight_share


def solution(mesh):
    return jax.shard_map(
        shards,
        mesh=mesh,
        in_specs=(
            P("gx", "gy", None, None, None),
            P(),
            P("gx", "gy", None, None, None),
            P("gx", "gy", None),
            P("gx", "gy", None, None),
            P("gx", "gy", None),
            P("gx", "gy", None, None, None),
            P("gx", "gy", None, None),
        ),
        out_specs=(P("gx", "gy", None, None, None), P("gx", "gy", None, None, None), P("gx", None)),
        check_vma=False,
    )
```

```python
import functools

import jax
import jax.numpy as jnp
from jax import lax
from jax.experimental import pallas as pl
from jax.experimental.pallas import tpu as pltpu
from jax.sharding import PartitionSpec as P


INTERPRET = False
BF = jnp.bfloat16
F32 = jnp.float32
VM = pltpu.MemorySpace.VMEM
HB = pltpu.MemorySpace.HBM
TABLES = ((1, 1, 2, 12), (1, 1, 12), (1, 1, 3, 2, 3), (1, 3, 1, 3))
FLAGS = ((1, 1, 3),)

PARITY = (1, 0, 1)
SHIFT = (1, 0, 0)
TAPS = [(e, f, g) for e in range(3) for f in range(3) for g in range(3)]


def tap_parity(tap):
    return PARITY[tap[0]] * 4 + PARITY[tap[1]] * 2 + PARITY[tap[2]]


def tap_shift(tap):
    return SHIFT[tap[0]] + 2 * SHIFT[tap[1]] + 4 * SHIFT[tap[2]]


def call(kernel, outs, args, spaces, scratch, flops, limit=4):
    nbytes = sum(a.size * a.dtype.itemsize for a in args)
    if not INTERPRET:
        args = [
            pltpu.with_memory_space_constraint(a, HB) if s == HB else a
            for a, s in zip(args, spaces)
        ]
    return pl.pallas_call(
        kernel,
        out_shape=outs,
        in_specs=[pl.BlockSpec(memory_space=s) for s in spaces],
        out_specs=jax.tree.map(lambda _: pl.BlockSpec(memory_space=VM), outs),
        scratch_shapes=scratch,
        compiler_params=pltpu.CompilerParams(vmem_limit_bytes=limit << 20),
        cost_estimate=pl.CostEstimate(flops=flops, bytes_accessed=nbytes, transcendentals=0),
        interpret=INTERPRET,
    )(*args)


def scalars(shapes):
    return [pltpu.SMEM(shape, jnp.int32) for shape in shapes] + [pltpu.SemaphoreType.DMA((8,))]


def fetch(sources, targets, sems):
    copies = [
        pltpu.make_async_copy(source, target, sems.at[n])
        for n, (source, target) in enumerate(zip(sources, targets))
    ]
    for copy in copies:
        copy.start()
    return copies


def parity_order():
    row = lax.broadcasted_iota(jnp.int32, (512, 512), 0)
    voxel = lax.broadcasted_iota(jnp.int32, (512, 512), 1)
    par, r, p, q = row >> 6, row >> 4 & 3, row >> 2 & 3, row & 3
    x = 2 * p + (par >> 2)
    y = 2 * q + (par >> 1 & 1)
    z = 2 * r + (par & 1)
    return jnp.where(voxel == x * 64 + y * 8 + z, 1.0, 0.0).astype(BF)


def split_kernel(valid_in, feat_in, weight_in, out, weight, feat, valid, sems):
    copies = fetch((valid_in, feat_in, weight_in), (valid, feat, weight), sems)
    order = parity_order()
    for copy in copies[:2]:
        copy.wait()
    for slot in range(3):
        rows = lax.dot_general(
            order, feat[0, 0, slot], (((1,), (1,)), ((), ())), preferred_element_type=F32
        )
        rows = (rows * valid[0, 0, slot].astype(F32)).astype(BF)
        for par in range(8):
            out[par, slot * 64 : slot * 64 + 64, :] = rows[par * 64 : par * 64 + 64]
    copies[2].wait()


def mask_kernel(valid_in, cot_in, masked, face_x, face_y, edge, cot, valid, sems):
    for copy in fetch((valid_in, cot_in), (valid, cot), sems):
        copy.wait()
    for slot in range(3):
        rows = cot[0, 0, slot].astype(F32) * valid[0, 0, slot].astype(F32)
        masked[slot] = rows.astype(BF)
        face_x[slot] = rows[0:16].astype(BF)
        face_y[slot] = jnp.concatenate(
            [rows[p * 16 : p * 16 + 4] for p in range(4)], axis=0
        ).astype(BF)
        edge[slot] = rows[0:8].astype(BF)


def row_ids():
    return lax.broadcasted_iota(jnp.int32, (64, 192), 0)


def gather_shift(first, second, axis):
    if axis == 2:
        return jnp.concatenate([first[16:], second[:16]], axis=0)
    step = 4 if axis == 0 else 1
    at = row_ids() // step % 4
    up = pltpu.roll(first, 64 - step, 0)
    wrap = pltpu.roll(second, 3 * step, 0)
    return jnp.where(at == 3, wrap, up)


def to_cube_order(cube, low, high):
    low[...] = cube[:, :128]
    high[:, 0:64] = cube[:, 128:]
    parts = []
    for r in range(4):
        take = pl.ds(r, 16, stride=4)
        parts.append(jnp.concatenate([low[take, :], high[take, :][:, 0:64]], axis=1))
    return jnp.concatenate(parts, axis=0)


def weight_kernel(
    lrules_in, lcodes_in, rrules_in, rcodes_in, split, masked, cot_x, cot_y, cot_xy,
    keep, send, shifts, cubes, grads, low, high, total, lrules, lcodes, rrules, rcodes, sems,
):
    copies = fetch(
        (lrules_in, lcodes_in, rrules_in, rcodes_in), (lrules, lcodes, rrules, rcodes), sems
    )
    zero = jnp.zeros((64, 192), F32)
    for group in range(16):
        cubes[group] = zero
    for slot in range(3):
        cubes[slot] = to_cube_order(masked[slot].astype(F32), low, high)
        from_x = cot_x[slot].astype(F32)
        from_y = cot_y[slot].astype(F32)
        from_xy = cot_xy[slot].astype(F32)
        for r in range(4):
            for n in range(4):
                put = slice(r * 16 + n, r * 16 + n + 1)
                cubes[4 + slot, put, :] = from_x[n * 4 + r : n * 4 + r + 1]
                put = slice(r * 16 + n * 4, r * 16 + n * 4 + 1)
                cubes[8 + slot, put, :] = from_y[n * 4 + r : n * 4 + r + 1]
            put = slice(r * 16, r * 16 + 1)
            cubes[12 + slot, put, :] = from_xy[r : r + 1]
    for entry in range(32):
        grads[entry] = zero
    for copy in copies:
        copy.wait()
    for e in range(12):
        at = lrules[0, 0, 0, e] * 8 + lcodes[0, 0, e]
        grads[at] += cubes[lrules[0, 0, 1, e]]
    for m in range(3):
        for e in range(3):
            at = rrules[0, 0, m, 0, e] * 8 + rcodes[0, m, 0, e]
            grads[at] += cubes[(m + 1) * 4 + rrules[0, 0, m, 1, e]]
    for slot in range(3):
        level = {}
        for u in range(2):
            for v in range(2):
                first = grads[slot * 8 + u + 2 * v]
                second = grads[slot * 8 + u + 2 * v + 4]
                level[u, v, 0] = first
                level[u, v, 1] = gather_shift(first, second, 2)
        after = {}
        for v in range(2):
            for w in range(2):
                after[0, v, w] = level[0, v, w]
                after[1, v, w] = gather_shift(level[0, v, w], level[1, v, w], 0)
        for u in range(2):
            for w in range(2):
                rows = slice(slot * 64, slot * 64 + 64)
                shifts[u + 4 * w, rows, :] = after[u, 0, w].astype(BF)
                shifts[u + 2 + 4 * w, rows, :] = gather_shift(
                    after[u, 0, w], after[u, 1, w], 1
                ).astype(BF)
    for index, tap in enumerate(TAPS):
        total[index * 192 : (index + 1) * 192, :] = lax.dot_general(
            split[tap_parity(tap)],
            shifts[tap_shift(tap)],
            (((0,), (0,)), ((), ())),
            preferred_element_type=F32,
        )
    here = lax.axis_index("gx")
    core = here % 2
    for m in range(16):
        other = m % 4 * 4 + m // 4
        for own in range(2):
            keeper = core if own else 1 - core
            block = ((here // 2) ^ jnp.where(keeper == 0, m, other)) * 2 + keeper
            start = pl.multiple_of(block * 162 // 8 * 8, 8)
            left = total[pl.ds(start, 168), 0:128]
            right = jnp.concatenate(
                [
                    total[pl.ds(start, 88), 128:192],
                    total[pl.ds(pl.multiple_of(start + 80, 8), 88), 128:192],
                ],
                axis=1,
            )
            if own:
                keep[m * 256 : m * 256 + 168, :] = left
                keep[m * 256 + 168 : m * 256 + 256, :] = right
            else:
                send[m * 256 : m * 256 + 168, :] = left.astype(BF)
                send[m * 256 + 168 : m * 256 + 256, :] = right.astype(BF)


def scatter_shift(first, second, axis):
    step = {2: 16, 0: 4, 1: 1}[axis]
    at = row_ids() // step % 4
    down = pltpu.roll(second, step, 0)
    out = pltpu.roll(second, 64 - 3 * step, 0)
    return first + jnp.where(at == 0, 0.0, down), jnp.where(at == 0, out, 0.0)


def forward_kernel(
    lrules_in, lcodes_in, rrules_in, rcodes_in, split, weight,
    local, to_x, to_y, regions, sums, pack, lrules, lcodes, rrules, rcodes, sems,
):
    copies = fetch(
        (lrules_in, lcodes_in, rrules_in, rcodes_in), (lrules, lcodes, rrules, rcodes), sems
    )
    for shift in range(8):
        acc = None
        for index, tap in enumerate(TAPS):
            if tap_shift(tap) == shift:
                part = lax.dot_general(
                    split[tap_parity(tap)],
                    weight[:, index * 192 : (index + 1) * 192],
                    (((1,), (1,)), ((), ())),
                    preferred_element_type=F32,
                )
                acc = part if acc is None else acc + part
        for slot in range(3):
            regions[slot * 8 + shift] = acc[slot * 64 : slot * 64 + 64]
    for slot in range(3):
        for bit, axis in ((1, 0), (2, 1), (4, 2)):
            for other in range(8):
                if other & bit:
                    continue
                inner, outer = scatter_shift(
                    regions[slot * 8 + other], regions[slot * 8 + other + bit], axis
                )
                regions[slot * 8 + other] = inner
                regions[slot * 8 + other + bit] = outer
    for entry in range(16):
        sums[entry] = jnp.zeros((64, 192), F32)
    for copy in copies:
        copy.wait()
    for e in range(12):
        at = jnp.minimum(lrules[0, 0, 0, e], 2) * 8 + lcodes[0, 0, e]
        sums[lrules[0, 0, 1, e]] += regions[at]
    for m in range(3):
        for e in range(3):
            at = jnp.minimum(rrules[0, 0, m, 0, e], 2) * 8 + rcodes[0, m, 0, e]
            sums[(m + 1) * 4 + rrules[0, 0, m, 1, e]] += regions[at]
    for t in range(3):
        local[t] = sums[t]
        pack[16:32, :] = jnp.zeros((16, 192), F32)
        for r in range(4):
            pack[r * 4 : r * 4 + 4, :] = sums[4 + t, r * 16 : r * 16 + 4, :]
            pack[16 + r : 17 + r, :] = sums[12 + t, r * 16 : r * 16 + 1, :]
            for p in range(4):
                to_y[t, r * 4 + p : r * 4 + p + 1, :] = sums[
                    8 + t, r * 16 + p * 4 : r * 16 + p * 4 + 1, :
                ]
        to_x[t] = pack[...].astype(BF)


def join_kernel(to_y, got_x, out, rows):
    for t in range(3):
        edge = got_x[t].astype(F32)
        rows[...] = to_y[t]
        for r in range(4):
            rows[r * 4 : r * 4 + 1, :] += edge[16 + r : 17 + r]
        out[t] = rows[...].astype(BF)


def output_kernel(valid_in, local, got_x, got_y, out, acc, low, high, valid, sems):
    for copy in fetch((valid_in,), (valid,), sems):
        copy.wait()
    for t in range(3):
        acc[...] = local[t]
        from_x = got_x[t].astype(F32)
        from_y = got_y[t].astype(F32)
        for r in range(4):
            acc[r * 16 : r * 16 + 4, :] += from_x[r * 4 : r * 4 + 4]
        for row in range(16):
            acc[row * 4 : row * 4 + 1, :] += from_y[row : row + 1]
        live = valid[0, 0, t].astype(F32)
        for r in range(4):
            rows = acc[r * 16 : r * 16 + 16, :] * live
            put = pl.ds(r, 16, stride=4)
            low[put, :] = rows[:, 0:128]
            high[put, :] = jnp.concatenate([rows[:, 128:192], rows[:, 128:192]], axis=1)
        out[0, 0, t, :, 0:128] = low[...].astype(BF)
        out[0, 0, t, :, 128:192] = high[:, 0:64].astype(BF)


def features_kernel(valid_in, shifts, weight, out, cubes, valid, sems):
    for copy in fetch((valid_in,), (valid,), sems):
        copy.wait()
    for par in range(8):
        acc = None
        for index, tap in enumerate(TAPS):
            if tap_parity(tap) == par:
                part = jnp.dot(
                    shifts[tap_shift(tap)],
                    weight[:, index * 192 : (index + 1) * 192],
                    preferred_element_type=F32,
                )
                acc = part if acc is None else acc + part
        for slot in range(3):
            live = valid[0, 0, slot].astype(F32)
            rows = acc[slot * 64 : slot * 64 + 64] * live
            cubes[slot, par * 64 : par * 64 + 64, :] = rows.astype(BF)
    order = parity_order()
    for slot in range(3):
        out[0, 0, slot] = lax.dot_general(
            cubes[slot], order, (((0,), (0,)), ((), ())), preferred_element_type=F32
        ).astype(BF)


def share_kernel(mine, other, out, rows):
    full = mine[...].astype(F32) + other[...].astype(F32)
    rows[:, 0:128] = full[0:168]
    rows[0:88, 128:192] = full[168:256, 0:64]
    rows[88:168, 128:192] = full[176:256, 64:128]
    offset = lax.axis_index("gx") % 4 * 2
    for case in range(4):
        @pl.when(offset == case * 2)
        def _(case=case):
            out[...] = rows[case * 2 : case * 2 + 162, :]


def swap(value, axis, size, bits):
    return lax.ppermute(value, axis, [(i, i ^ bits) for i in range(size)])


def step(value, axis, sign):
    size = lax.axis_size(axis)
    route = [(i, i + sign) for i in range(size) if 0 <= i + sign < size]
    return lax.ppermute(value, axis, route)


def split_sum_kernel(count, mine, *refs):
    got, first, rest = refs[:count], refs[count], refs[count + 1 :]
    size = first.shape[0]
    for d in range(4):
        rows = slice(d * size, d * size + size)
        full = mine[rows, :]
        for ref in got:
            full = full + ref[rows, :].astype(F32)
        if d == 0:
            first[...] = full
        else:
            rest[d - 1][...] = full.astype(BF)


def split_sum(mine, got, limit):
    size = mine.shape[0] // 4
    outs = (jax.ShapeDtypeStruct((size, 128), F32),) + (jax.ShapeDtypeStruct((size, 128), BF),) * 3
    args = (mine, *got)
    kernel = functools.partial(split_sum_kernel, len(got))
    first, *rest = call(kernel, outs, args, (VM,) * len(args), [], 0, limit)
    return first, rest


def sum_kernel(first, one, two, three, out):
    total = first[...].astype(F32) + one[...].astype(F32)
    out[...] = (total + (two[...].astype(F32) + three[...].astype(F32))).astype(BF)


def sum_of(values):
    return call(sum_kernel, jax.ShapeDtypeStruct((256, 128), BF), values, (VM,) * 4, [], 0, 2)


def turns(parts, first_bits, second_bits):
    got = {}
    for d in (2, 3, 1):
        route = [(i, i ^ ((second_bits if i % 2 else first_bits) * d)) for i in range(32)]
        got[d] = lax.ppermute(parts[d - 1], "gx", route)
    return [got[1], got[2], got[3]]


def together(*values):
    return lax.optimization_barrier(values)


def shards(
    features, weight, cotangent, valid, local_rules, local_codes, remote_rules, remote_codes
):
    rules = (
        local_rules,
        local_codes,
        jnp.transpose(remote_rules, (0, 1, 3, 2, 4)),
        jnp.transpose(remote_codes, (0, 2, 1, 3)),
    )
    weight = weight.T
    features = jnp.swapaxes(features, 3, 4)
    shape = jax.ShapeDtypeStruct
    flops = 2 * 27 * 192**3
    masked, face_x, face_y, edge = call(
        mask_kernel,
        (shape((3, 64, 192), BF),) + (shape((3, 16, 192), BF),) * 2 + (shape((3, 8, 192), BF),),
        (valid, cotangent),
        (HB, HB),
        [pltpu.VMEM((1, 1, 3, 64, 192), BF)] + scalars(FLAGS),
        0,
        2,
    )
    cot_y = step(face_y, "gy", -1)
    columns = lax.axis_size("gy")
    route = [
        (i * columns + j, (i - 1) * columns + j - 1)
        for i in range(1, lax.axis_size("gx"))
        for j in range(1, columns)
    ]
    cot_xy = lax.ppermute(edge, ("gx", "gy"), route)
    cot_x = step(face_x, "gx", -1)
    split, weight = call(
        split_kernel,
        (shape((8, 192, 192), BF), shape((192, 5184), BF)),
        (valid, together(features, edge)[0], weight),
        (HB,) * 3,
        [pltpu.VMEM((1, 1, 3, 192, 512), BF)] + scalars(FLAGS),
        flops,
        10,
    )
    local, to_x, to_y = call(
        forward_kernel,
        (shape((3, 64, 192), F32), shape((3, 32, 192), BF), shape((3, 16, 192), F32)),
        (*rules, split, weight),
        (HB,) * 4 + (VM,) * 2,
        [pltpu.VMEM((24, 64, 192), F32), pltpu.VMEM((16, 64, 192), F32), pltpu.VMEM((32, 192), F32)]
        + scalars(TABLES),
        flops,
        12,
    )
    split, local, to_x, to_y = together(split, local, to_x, to_y)
    keep, send, shifts = call(
        weight_kernel,
        (shape((4096, 128), F32), shape((4096, 128), BF), shape((8, 192, 192), BF)),
        (*rules, split, masked, cot_x, cot_y, cot_xy),
        (HB,) * 4 + (VM,) * 5,
        [pltpu.VMEM((16, 64, 192), F32), pltpu.VMEM((32, 64, 192), F32)]
        + [pltpu.VMEM((64, 128), F32)] * 2
        + [pltpu.VMEM((5184, 192), F32)]
        + scalars(TABLES),
        flops,
        18,
    )
    arrived = swap(send, "gx", 32, 1)
    first, rest = split_sum(keep, [arrived], 8)
    rest, shifts, to_x = together(rest, shifts, to_x)
    arrived = turns(rest, 8, 2)
    got_x = step(to_x, "gx", 1)
    features_grad = call(
        features_kernel,
        shape((1, 1, 3, 192, 512), BF),
        (valid, shifts, weight),
        (HB, VM, VM),
        [pltpu.VMEM((3, 512, 192), BF)] + scalars(FLAGS),
        flops,
        12,
    )
    arrived, features_grad = together(arrived, features_grad)
    first, rest = split_sum(first, arrived, 4)
    part = sum_of((first, *turns(rest, 2, 8)))
    part, to_y = together(part, to_y)
    got = [swap(part, "gy", 8, d) for d in (1, 2, 3)]
    joined = call(
        join_kernel, shape((3, 16, 192), BF), (to_y, got_x), (VM, VM),
        [pltpu.VMEM((16, 192), F32)], 0, 2,
    )
    got_y = step(joined, "gy", 1)
    part = sum_of((part, *got))
    part, local = together(part, local)
    other = swap(part, "gy", 8, 4)
    output = call(
        output_kernel,
        shape((1, 1, 3, 64, 192), BF),
        (valid, local, got_x, got_y),
        (HB,) + (VM,) * 3,
        [pltpu.VMEM((64, 192), F32)] + [pltpu.VMEM((64, 128), F32)] * 2 + scalars(FLAGS),
        0,
    )
    other, output = together(other, output)
    weight_share = call(
        share_kernel,
        shape((162, 192), F32),
        (part, other),
        (VM, VM),
        [pltpu.VMEM((168, 192), F32)],
        0,
        2,
    )
    features_grad = jnp.swapaxes(features_grad, 3, 4)
    return output, features_grad, weight_share


def solution(mesh):
    return jax.shard_map(
        shards,
        mesh=mesh,
        in_specs=(
            P("gx", "gy", None, None, None),
            P(),
            P("gx", "gy", None, None, None),
            P("gx", "gy", None),
            P("gx", "gy", None, None),
            P("gx", "gy", None),
            P("gx", "gy", None, None, None),
            P("gx", "gy", None, None),
        ),
        out_specs=(P("gx", "gy", None, None, None), P("gx", "gy", None, None, None), P("gx", None)),
        check_vma=False,
    )
```
